32 devices in a mesh: station: 8 (over y, x, core), tm: 4 (over z).
Axes of the slice: x: 2, y: 2, z: 4, core: 2. Of those that a mesh axis runs over, the one named last changes fastest.
Arguments:
- samples: bfloat16 [64, 256, 2048], P('tm', 'station'), may hold values from -6 to 6
- history: bfloat16 [15, 256, 2048], P(None, 'station'), may hold values from -6 to 6
- taps: float32 [16, 2048], replicated, may hold values from -0.03125 to 0.03125
Outputs:
- visibility: float32 [1024, 2, 256, 256], P(('station', 'tm'))
- beam_power: float32 [64, 1024], P('tm', 'station')
The draws below stay inside these ranges and needn't reach their ends.
All inputs are finite; a program needn't handle non-finite values.
Results may differ from the reference program's by a relative error of at most 0.0095.
Values may be sent and summed in bfloat16 or wider, within the bound.
A program may use at most 128 MiB of HBM per device.

```python
import math
import jax
import jax.numpy as jnp
from jax import lax

STATIONS = 128
NCHAN = 1024
TAPS = 16
SPEC_DEV = 16
INPUTS = 256
NSPEC = 64
N_TM = 4


def levels(stream_key, extent, pieces, low, high):
    loudness = 1.0
    for axis_at, parts in pieces:
        draws = jax.random.uniform(jax.random.fold_in(jax.random.fold_in(stream_key, 6), axis_at), (parts,), jnp.float32, low / len(pieces), high / len(pieces))
        loudness = loudness * jnp.repeat(jnp.exp(draws), extent[axis_at] // parts).reshape((-1,) + (1,) * (len(extent) - 1 - axis_at))
    return loudness


def gaussian(own_key, shape, spread, most, split=(), kind=jnp.bfloat16):
    drawn = jax.random.normal(own_key, shape, jnp.float32) * spread
    if len(split) > 0:
        drawn = levels(own_key, shape, split, -0.22, 0.18) * drawn
    return jnp.clip(drawn, min=-most, max=most).astype(kind)


def setup_inputs(seed: int = 0) -> dict:
    key_list = jax.random.split(jax.random.key(seed), 4)
    samples = gaussian(key_list[0], (NSPEC, INPUTS, 2 * NCHAN), 1.0, 6.0, ((0, 4), (1, 8)))
    history = gaussian(key_list[1], (TAPS - 1, INPUTS, 2 * NCHAN), 1.0, 6.0, ((1, 8),))
    taps = gaussian(key_list[2], (TAPS, 2 * NCHAN), (TAPS * 2 * NCHAN) ** -0.5, 0.03125, (), jnp.float32)
    return dict(samples=samples, history=history, taps=taps)


def dft_table(frame_len, channels):
    sample_index = jnp.arange(frame_len, dtype=jnp.int32)
    channel_index = jnp.arange(channels, dtype=jnp.int32)
    phases = (sample_index[:, None] * channel_index[None, :]) % frame_len
    angles = phases.astype(jnp.float32) * (2.0 * math.pi / frame_len)
    dft_values = jnp.stack([jnp.cos(angles), -jnp.sin(angles)], axis=2)
    return dft_values.reshape(frame_len, 2 * channels).astype(jnp.bfloat16)


def filter_frames(extended, taps, frames_out):
    span_taps = taps.shape[0]
    running = jnp.zeros((frames_out,) + extended.shape[1:], jnp.float32)
    for tap_index in range(span_taps):
        offset = span_taps - 1 - tap_index
        running = running + taps[tap_index][None, None, :] * extended[offset:offset + frames_out].astype(jnp.float32)
    return running.astype(jnp.bfloat16)


def beam_power_of(spectra):
    values = spectra.astype(jnp.float32)
    return jnp.sum(values * values, axis=(1, 3)) * (1.0 / spectra.shape[1])


def correlate(spectra, norm_scale):
    values = spectra.astype(jnp.float32)
    rotated = jnp.stack([-values[..., 1], values[..., 0]], axis=-1)
    real_part = jnp.einsum('tacp,tbcp->cab', values, values, precision=lax.Precision.HIGHEST) * norm_scale
    imag_part = jnp.einsum('tacp,tbcp->cab', rotated, values, precision=lax.Precision.HIGHEST) * norm_scale
    return real_part, imag_part


def reference(samples, history, taps):
    frame_len = 2 * NCHAN
    inputs = 2 * STATIONS
    dft_values = dft_table(frame_len, NCHAN).astype(jnp.float32)
    norm_scale = 1.0 / (SPEC_DEV * N_TM)
    blocks = samples.reshape(N_TM, SPEC_DEV, inputs, frame_len)

    def advance(state_pair, time_block):
        prior_frames, running = state_pair
        extended = jnp.concatenate([prior_frames, time_block], axis=0)
        weighted = filter_frames(extended, taps, SPEC_DEV)
        weighted = lax.optimization_barrier(weighted)
        spectra = jnp.dot(weighted.reshape(SPEC_DEV * inputs, frame_len).astype(jnp.float32), dft_values,
                          precision=lax.Precision.HIGHEST, preferred_element_type=jnp.float32)
        spectra = lax.optimization_barrier(spectra.astype(jnp.bfloat16))
        spectra = spectra.reshape(SPEC_DEV, inputs, NCHAN, 2)
        power_rows = beam_power_of(spectra)
        real_part, imag_part = correlate(spectra, norm_scale)
        partial_value = jnp.stack([real_part, imag_part], axis=1).astype(jnp.bfloat16)
        partial_value = lax.optimization_barrier(partial_value)
        running = running + partial_value.astype(jnp.float32)
        return (time_block[SPEC_DEV - (TAPS - 1):], running), power_rows

    initial_sum = jnp.zeros((NCHAN, 2, inputs, inputs), jnp.float32)
    final_pair, powers = lax.scan(advance, (history, initial_sum), blocks)
    return final_pair[1], powers.reshape(SPEC_DEV * N_TM, NCHAN)
```

```python
import functools
import math

import jax
import jax.numpy as jnp
import numpy as np
from jax import lax
from jax.experimental import pallas as pl
from jax.experimental.pallas import tpu as pltpu
from jax.sharding import PartitionSpec as P

MESH = pl.DeviceIdType.MESH
LANES = 128
VMEM_LIMIT = 44 * 1024 * 1024


def dft_table(stations, blocks, own, frame_len):
    channel = np.arange(stations * blocks * own).reshape(stations, blocks, own)
    channel = channel.transpose(1, 0, 2).reshape(-1)
    phase = channel[:, None] * np.arange(frame_len)[None, :] % frame_len
    angle = phase.astype(np.float32) * np.float32(2.0 * math.pi / frame_len)
    parts = np.stack([np.cos(angle), -np.sin(angle)], axis=0)
    parts = parts.reshape(2, blocks * stations, own, frame_len).transpose(1, 0, 2, 3)
    return jnp.asarray(parts.reshape(-1, frame_len).astype(jnp.bfloat16))


def channel_rows(wide, channel, stations, blocks, own, local):
    slots = LANES // local
    rows = 2 * blocks
    lane = lax.broadcasted_iota(jnp.int32, (rows, LANES), 1) // local
    sign = jnp.where(
        lax.broadcasted_iota(jnp.int32, (rows, stations * local), 0) < blocks, 1.0, -1.0
    )
    halves = []
    for h in range(stations // slots):
        parts = [
            wide[h * slots + s, pl.ds(channel, rows, stride=own), :] for s in range(slots)
        ]
        tiles = []
        for t in range(slots):
            tile = None
            for s in range(slots):
                shift = (s - t) % slots * local
                moved = parts[s] if shift == 0 else pltpu.roll(parts[s], shift, 1)
                tile = moved if tile is None else jnp.where(lane == s, moved, tile)
            tiles.append(tile)
        halves.append(tiles)
    flat, turned = [], []
    for t in range(slots):
        full = jnp.concatenate([half[t] for half in halves], axis=1)
        flat.append(full)
        turned.append(pltpu.roll(full, blocks, 0) * sign)
    flat = jnp.concatenate(flat, axis=0).astype(jnp.bfloat16)
    turned = jnp.concatenate(turned, axis=0).astype(jnp.bfloat16)
    return flat, turned


def spectra_kernel(
    stations, blocks, own, local, frames, span,
    samples, history, taps_hbm, table_hbm,
    both, powers,
    ext, taps, table, weighted, spec, got, wide, power, power_got,
    load_sem, halo_send, halo_recv, spec_send, spec_recv, power_send, power_recv,
):
    me_s, me_t = lax.axis_index("station"), lax.axis_index("tm")
    dests = stations * blocks
    per = LANES // local
    chunks = frames // per
    frame_len = samples.shape[2]
    hist = span - 1
    first = me_t == 0
    last = me_t == blocks - 1

    load_table = pltpu.make_async_copy(table_hbm, table, load_sem.at[0])
    load_own = pltpu.make_async_copy(samples, ext.at[pl.ds(hist, frames)], load_sem.at[1])
    load_hist = pltpu.make_async_copy(history, ext.at[pl.ds(0, hist)], load_sem.at[2])

    load_taps = pltpu.make_async_copy(taps_hbm, taps, load_sem.at[3])

    barrier = pltpu.get_barrier_semaphore()

    def greet(i, carry):
        other = lax.rem(me_s * blocks + me_t + i, dests)
        pl.semaphore_signal(
            barrier,
            inc=1,
            device_id=(other // blocks, lax.rem(other, blocks)),
            device_id_type=MESH,
        )
        return carry

    lax.fori_loop(1, dests, greet, 0)
    load_own.start()
    pl.when(first)(load_hist.start)
    load_taps.start()
    load_table.start()
    pl.semaphore_wait(barrier, dests - 1)

    def halo(k, target):
        return pltpu.make_async_remote_copy(
            src_ref=samples.at[pl.ds(k * per, per)],
            dst_ref=ext.at[pl.ds(hist + frames + k * per, per)],
            send_sem=halo_send.at[k],
            recv_sem=halo_recv.at[k],
            device_id=(me_s, target),
            device_id_type=MESH,
        )

    @pl.when(jnp.logical_not(first))
    def _():
        for k in range(chunks):
            halo(k, me_t - 1).start()

    load_own.wait()
    pl.when(first)(load_hist.wait)
    load_taps.wait()
    load_table.wait()

    def filter_chunk(start):
        def tile(i, carry):
            lanes = pl.ds(pl.multiple_of(i * LANES, LANES), LANES)
            sums = [None] * per
            for e in range(per + span - 1):
                x = ext[start + e, :, lanes].astype(jnp.float32)
                for j in range(per):
                    tap = j + span - 1 - e
                    if 0 <= tap < span:
                        term = taps[tap : tap + 1, lanes] * x
                        sums[j] = term if sums[j] is None else sums[j] + term
            for j in range(per):
                weighted[j * local : (j + 1) * local, lanes] = sums[j].astype(jnp.bfloat16)
            return carry

        lax.fori_loop(0, frame_len // LANES, tile, 0)

    def send(job, plane):
        k = lax.rem(job, chunks)
        block = jnp.where(job < chunks, 0, me_t + 1)

        def one(i, carry):
            s = lax.rem(me_s + i, stations)
            here = jnp.logical_and(i == 0, plane == me_t)
            piece = spec.at[job, plane * stations + s]

            @pl.when(here)
            def _():
                pltpu.make_async_copy(piece, got.at[k, block, me_s], spec_recv.at[k]).start()

            @pl.when(jnp.logical_not(here))
            def _():
                pltpu.make_async_remote_copy(
                    src_ref=piece,
                    dst_ref=got.at[k, block, me_s],
                    send_sem=spec_send.at[job],
                    recv_sem=spec_recv.at[k],
                    device_id=(s, plane),
                    device_id_type=MESH,
                ).start()

            return carry

        lax.fori_loop(0, stations, one, 0)

    def work(job, carry):
        @pl.when(job >= chunks)
        def _():
            halo(job - chunks, me_t).wait_recv()

        @pl.when(job == 2 * chunks - 1)
        def _():
            def older(old, carry):
                def plane_of(plane, carry):
                    send(old, plane)
                    return carry

                return lax.fori_loop(0, me_t, plane_of, carry)

            lax.fori_loop(chunks, 2 * chunks - 1, older, 0)

        filter_chunk(job * per)

        def planes(i, carry):
            plane = blocks - 1 - i
            depth = stations * 2 * own
            out = lax.dot_general(
                table[pl.ds(pl.multiple_of(plane * depth, depth), depth), :],
                weighted[...],
                (((1,), (1,)), ((), ())),
                preferred_element_type=jnp.float32,
            )
            out = out.astype(jnp.bfloat16).reshape(stations, 2 * own, LANES)
            spec[job, pl.ds(plane * stations, stations)] = out
            now = jnp.logical_or(plane >= me_t, job == 2 * chunks - 1)
            pl.when(now)(lambda: send(job, plane))
            return carry

        lax.fori_loop(0, blocks, planes, 0)
        return carry

    low = jnp.where(first, 0, chunks)
    high = jnp.where(last, chunks, 2 * chunks)
    lax.fori_loop(low, high, work, 0)

    power[...] = jnp.zeros_like(power)

    def arrange(k, carry):
        pltpu.make_async_copy(got.at[k], got.at[k], spec_recv.at[k]).wait()

        def fill(s, carry):
            for b in range(blocks):
                for p in range(2):
                    wide[s, (p * blocks + b) * own : (p * blocks + b + 1) * own, :] = got[
                        k, b, s, p * own : (p + 1) * own, :
                    ].astype(jnp.float32)
            return carry

        lax.fori_loop(0, stations, fill, 0)

        half = blocks * own
        total = jnp.zeros((half, LANES), jnp.float32)
        for s in range(stations):
            re, im = wide[s, :half, :], wide[s, half:, :]
            total = total + (re * re + im * im)
        frame = lax.broadcasted_iota(jnp.int32, (frames, LANES), 0) - k * per
        pick = (lax.broadcasted_iota(jnp.int32, (frames, LANES), 1) // local == frame).astype(
            jnp.float32
        )
        power[...] += lax.dot_general(
            pick,
            total,
            (((1,), (1,)), ((), ())),
            precision=lax.Precision.HIGHEST,
            preferred_element_type=jnp.float32,
        )

        @pl.when(k == chunks - 1)
        def _():
            power_got[me_t] = power[...]
            for i in range(1, blocks):
                power_copy(i).start()

        def channel(c, carry):
            flat, turned = channel_rows(wide, c, stations, blocks, own, local)
            depth = 2 * blocks * per
            rows = pl.ds(pl.multiple_of(k * depth, depth), depth)
            both[c, rows, : stations * local] = flat
            both[c, rows, stations * local :] = turned
            return carry

        lax.fori_loop(0, own, channel, 0)
        return carry

    def power_copy(i):
        return pltpu.make_async_remote_copy(
            src_ref=power,
            dst_ref=power_got.at[me_t],
            send_sem=power_send.at[i],
            recv_sem=power_recv.at[i],
            device_id=(me_s, lax.rem(me_t + i, blocks)),
            device_id_type=MESH,
        )

    lax.fori_loop(0, chunks, arrange, 0)

    for i in range(1, blocks):
        power_copy(i).wait()
    powers[...] = power_got[...]

    def drain(job, carry):
        sent = spec.at[job, pl.ds(0, dests - 1)]
        pltpu.make_async_copy(sent, sent, spec_send.at[job]).wait()
        return carry

    lax.fori_loop(low, high, drain, 0)

    @pl.when(jnp.logical_not(first))
    def _():
        for k in range(chunks):
            halo(k, me_t - 1).wait_send()


def correlate_kernel(blocks, own, scale, both, powers, vis, power):
    inputs = both.shape[2] // 2
    step = pl.program_id(0)

    @pl.when(step == 0)
    def _():
        me = lax.axis_index("tm")
        wide = powers.shape[2]
        row = lax.broadcasted_iota(jnp.int32, (wide, wide), 0)
        col = lax.broadcasted_iota(jnp.int32, (wide, wide), 1)
        total = jnp.zeros(power.shape, jnp.float32)
        for b in range(blocks):
            move = jnp.logical_and(row - me * own == col - b * own, col // own == b)
            total = total + lax.dot_general(
                powers[b],
                move.astype(jnp.float32),
                (((1,), (0,)), ((), ())),
                precision=lax.Precision.HIGHEST,
                preferred_element_type=jnp.float32,
            )
        power[...] = total * (1.0 / inputs)

    for g in range(vis.shape[0]):
        out = lax.dot_general(
            both[g, :, :inputs],
            both[g],
            (((0,), (0,)), ((), ())),
            preferred_element_type=jnp.float32,
        )
        vis[g, 0] = out[:, :inputs] * scale
        vis[g, 1] = out[:, inputs:] * scale


def body(samples, history, taps):
    frames, local, frame_len = samples.shape
    span = taps.shape[0]
    stations, blocks = lax.axis_size("station"), lax.axis_size("tm")
    dests = stations * blocks
    inputs = stations * local
    own = frame_len // 2 // dests
    per = LANES // local
    chunks = frames // per
    depth = 2 * frames * blocks
    table = dft_table(stations, blocks, own, frame_len)
    hbm = pl.BlockSpec(memory_space=pltpu.HBM)
    vmem = pl.BlockSpec(memory_space=pltpu.VMEM)
    both, powers = pl.pallas_call(
        functools.partial(spectra_kernel, stations, blocks, own, local, frames, span),
        in_specs=[hbm, hbm, hbm, hbm],
        out_specs=[vmem, vmem],
        out_shape=[
            jax.ShapeDtypeStruct((own, depth, 2 * inputs), jnp.bfloat16),
            jax.ShapeDtypeStruct((blocks, frames, blocks * own), jnp.float32),
        ],
        scratch_shapes=[
            pltpu.VMEM((span - 1 + 2 * frames, local, frame_len), jnp.bfloat16),
            pltpu.VMEM(taps.shape, jnp.float32),
            pltpu.VMEM(table.shape, jnp.bfloat16),
            pltpu.VMEM((LANES, frame_len), jnp.bfloat16),
            pltpu.VMEM((2 * chunks, dests, 2 * own, LANES), jnp.bfloat16),
            pltpu.VMEM((chunks, blocks, stations, 2 * own, LANES), jnp.bfloat16),
            pltpu.VMEM((stations, 2 * blocks * own, LANES), jnp.float32),
            pltpu.VMEM((frames, blocks * own), jnp.float32),
            pltpu.VMEM((blocks, frames, blocks * own), jnp.float32),
            pltpu.SemaphoreType.DMA((4,)),
            pltpu.SemaphoreType.DMA((chunks,)),
            pltpu.SemaphoreType.DMA((chunks,)),
            pltpu.SemaphoreType.DMA((2 * chunks,)),
            pltpu.SemaphoreType.DMA((chunks,)),
            pltpu.SemaphoreType.DMA((blocks,)),
            pltpu.SemaphoreType.DMA((blocks,)),
        ],
        compiler_params=pltpu.CompilerParams(
            collective_id=0, has_side_effects=True, vmem_limit_bytes=VMEM_LIMIT
        ),
        cost_estimate=pl.CostEstimate(
            flops=8 * frames * local * frame_len * dests * own,
            bytes_accessed=8 * samples.size + table.size * 2,
            transcendentals=0,
        ),
    )(samples, history, taps, table)

    group = math.gcd(own, 4)
    visibility, power = pl.pallas_call(
        functools.partial(correlate_kernel, blocks, own, 1.0 / (frames * blocks)),
        grid=(own // group,),
        in_specs=[
            pl.BlockSpec((group, depth, 2 * inputs), lambda c: (c, 0, 0)),
            pl.BlockSpec(powers.shape, lambda c: (0, 0, 0)),
        ],
        out_specs=[
            pl.BlockSpec((group, 2, inputs, inputs), lambda c: (c, 0, 0, 0)),
            pl.BlockSpec((frames, blocks * own), lambda c: (0, 0)),
        ],
        out_shape=[
            jax.ShapeDtypeStruct((own, 2, inputs, inputs), jnp.float32),
            jax.ShapeDtypeStruct((frames, blocks * own), jnp.float32),
        ],
        compiler_params=pltpu.CompilerParams(vmem_limit_bytes=24 * 1024 * 1024),
    )(both, powers)
    return visibility, power


def solution(mesh):
    return jax.shard_map(
        body,
        mesh=mesh,
        in_specs=(P("tm", "station", None), P(None, "station", None), P()),
        out_specs=(P(("station", "tm"), None, None, None), P("tm", "station")),
        check_vma=False,
    )
```

```python
import functools
import math

import jax
import jax.numpy as jnp
import numpy as np
from jax import lax
from jax.experimental import pallas as pl
from jax.experimental.pallas import tpu as pltpu
from jax.sharding import PartitionSpec as P

MESH = pl.DeviceIdType.MESH
LANES = 128
VMEM_LIMIT = 44 * 1024 * 1024


def dft_table(stations, blocks, own, frame_len):
    channel = np.arange(stations * blocks * own).reshape(stations, blocks, own)
    channel = channel.transpose(1, 0, 2).reshape(-1)
    phase = channel[:, None] * np.arange(frame_len)[None, :] % frame_len
    angle = phase.astype(np.float32) * np.float32(2.0 * math.pi / frame_len)
    parts = np.stack([np.cos(angle), -np.sin(angle)], axis=0)
    parts = parts.reshape(2, blocks * stations, own, frame_len).transpose(1, 0, 2, 3)
    return jnp.asarray(parts.reshape(-1, frame_len).astype(jnp.bfloat16))


def channel_rows(wide, channel, stations, blocks, own, local):
    slots = LANES // local
    rows = 2 * blocks
    lane = lax.broadcasted_iota(jnp.int32, (rows, LANES), 1) // local
    sign = jnp.where(
        lax.broadcasted_iota(jnp.int32, (rows, stations * local), 0) < blocks, 1.0, -1.0
    )
    halves = []
    for h in range(stations // slots):
        parts = [
            wide[h * slots + s, pl.ds(channel, rows, stride=own), :] for s in range(slots)
        ]
        tiles = []
        for t in range(slots):
            tile = None
            for s in range(slots):
                shift = (s - t) % slots * local
                moved = parts[s] if shift == 0 else pltpu.roll(parts[s], shift, 1)
                tile = moved if tile is None else jnp.where(lane == s, moved, tile)
            tiles.append(tile)
        halves.append(tiles)
    flat, turned = [], []
    for t in range(slots):
        full = jnp.concatenate([half[t] for half in halves], axis=1)
        flat.append(full)
        turned.append(pltpu.roll(full, blocks, 0) * sign)
    flat = jnp.concatenate(flat, axis=0).astype(jnp.bfloat16)
    turned = jnp.concatenate(turned, axis=0).astype(jnp.bfloat16)
    return flat, turned


def spectra_kernel(
    stations, blocks, own, local, frames, span,
    samples, history, taps_hbm, table_hbm,
    both, powers,
    ext, taps, table, weighted, spec, got, wide, power, power_got,
    load_sem, table_sem, halo_send, halo_recv, spec_send, spec_recv, power_send, power_recv,
):
    me_s, me_t = lax.axis_index("station"), lax.axis_index("tm")
    dests = stations * blocks
    per = LANES // local
    chunks = frames // per
    frame_len = samples.shape[2]
    hist = span - 1
    first = me_t == 0
    last = me_t == blocks - 1

    load_own = pltpu.make_async_copy(samples, ext.at[pl.ds(hist, frames)], load_sem.at[0])
    load_hist = pltpu.make_async_copy(history, ext.at[pl.ds(0, hist)], load_sem.at[1])

    load_taps = pltpu.make_async_copy(taps_hbm, taps, load_sem.at[2])

    depth = stations * 2 * own

    def load_table(plane):
        rows = pl.ds(pl.multiple_of(plane * depth, depth), depth)
        return pltpu.make_async_copy(table_hbm.at[rows], table.at[rows], table_sem.at[plane])

    load_own.start()
    pl.when(first)(load_hist.start)
    load_taps.start()

    @pl.when(jnp.logical_not(last))
    def _():
        for plane in reversed(range(blocks)):
            load_table(plane).start()

    barrier = pltpu.get_barrier_semaphore()

    def greet(i, carry):
        other = lax.rem(me_s * blocks + me_t + i, dests)
        pl.semaphore_signal(
            barrier,
            inc=1,
            device_id=(other // blocks, lax.rem(other, blocks)),
            device_id_type=MESH,
        )
        return carry

    lax.fori_loop(1, dests, greet, 0)
    load_own.wait()
    load_taps.wait()

    def filter_chunk(start):
        def tile(i, carry):
            lanes = pl.ds(pl.multiple_of(i * LANES, LANES), LANES)
            sums = [None] * per
            for e in range(per + span - 1):
                x = ext[start + e, :, lanes].astype(jnp.float32)
                for j in range(per):
                    tap = j + span - 1 - e
                    if 0 <= tap < span:
                        term = taps[tap : tap + 1, lanes] * x
                        sums[j] = term if sums[j] is None else sums[j] + term
            for j in range(per):
                weighted[j * local : (j + 1) * local, lanes] = sums[j].astype(jnp.bfloat16)
            return carry

        lax.fori_loop(0, frame_len // LANES, tile, 0)

    @pl.when(first)
    def _():
        load_hist.wait()
        filter_chunk(0)

    pl.semaphore_wait(barrier, dests - 1)

    def halo(k, target):
        return pltpu.make_async_remote_copy(
            src_ref=samples.at[pl.ds(k * per, per)],
            dst_ref=ext.at[pl.ds(hist + frames + k * per, per)],
            send_sem=halo_send.at[k],
            recv_sem=halo_recv.at[k],
            device_id=(me_s, target),
            device_id_type=MESH,
        )

    @pl.when(jnp.logical_not(first))
    def _():
        for k in range(chunks):
            halo(k, me_t - 1).start()

    def send(job, plane):
        k = lax.rem(job, chunks)
        block = jnp.where(job < chunks, 0, me_t + 1)

        def one(i, carry):
            s = lax.rem(me_s + i, stations)
            here = jnp.logical_and(i == 0, plane == me_t)
            piece = spec.at[job, plane * stations + s]

            @pl.when(here)
            def _():
                pltpu.make_async_copy(piece, got.at[k, block, me_s], spec_recv.at[k]).start()

            @pl.when(jnp.logical_not(here))
            def _():
                pltpu.make_async_remote_copy(
                    src_ref=piece,
                    dst_ref=got.at[k, block, me_s],
                    send_sem=spec_send.at[job],
                    recv_sem=spec_recv.at[k],
                    device_id=(s, plane),
                    device_id_type=MESH,
                ).start()

            return carry

        lax.fori_loop(0, stations, one, 0)

    low = jnp.where(first, 0, chunks)
    high = jnp.where(last, chunks, 2 * chunks)

    def work(job, carry):
        @pl.when(job >= chunks)
        def _():
            halo(job - chunks, me_t).wait_recv()

        @pl.when(job == 2 * chunks - 1)
        def _():
            def older(old, carry):
                def plane_of(plane, carry):
                    send(old, plane)
                    return carry

                return lax.fori_loop(0, me_t, plane_of, carry)

            lax.fori_loop(chunks, 2 * chunks - 1, older, 0)

        pl.when(job > 0)(lambda: filter_chunk(job * per))

        def planes(i, carry):
            plane = blocks - 1 - i
            pl.when(job == low)(load_table(plane).wait)
            out = lax.dot_general(
                table[pl.ds(pl.multiple_of(plane * depth, depth), depth), :],
                weighted[...],
                (((1,), (1,)), ((), ())),
                preferred_element_type=jnp.float32,
            )
            out = out.astype(jnp.bfloat16).reshape(stations, 2 * own, LANES)
            spec[job, pl.ds(plane * stations, stations)] = out
            near = jnp.logical_and(job < chunks - 1, plane == me_t + 1)
            now = jnp.where(job == 2 * chunks - 1, True, jnp.logical_and(plane >= me_t, jnp.logical_not(near)))
            pl.when(now)(lambda: send(job, plane))
            return carry

        lax.fori_loop(0, blocks, planes, 0)

        @pl.when(job == chunks - 1)
        def _():
            def near(old, carry):
                send(old, me_t + 1)
                return carry

            lax.fori_loop(0, chunks - 1, near, 0)

        return carry

    lax.fori_loop(low, high, work, 0)

    power[...] = jnp.zeros_like(power)

    def arrange(k, carry):
        pltpu.make_async_copy(got.at[k], got.at[k], spec_recv.at[k]).wait()

        def fill(s, carry):
            for b in range(blocks):
                for p in range(2):
                    wide[s, (p * blocks + b) * own : (p * blocks + b + 1) * own, :] = got[
                        k, b, s, p * own : (p + 1) * own, :
                    ].astype(jnp.float32)
            return carry

        lax.fori_loop(0, stations, fill, 0)

        half = blocks * own
        total = jnp.zeros((half, LANES), jnp.float32)
        for s in range(stations):
            re, im = wide[s, :half, :], wide[s, half:, :]
            total = total + (re * re + im * im)
        frame = lax.broadcasted_iota(jnp.int32, (frames, LANES), 0) - k * per
        pick = (lax.broadcasted_iota(jnp.int32, (frames, LANES), 1) // local == frame).astype(
            jnp.float32
        )
        power[...] += lax.dot_general(
            pick,
            total,
            (((1,), (1,)), ((), ())),
            precision=lax.Precision.HIGHEST,
            preferred_element_type=jnp.float32,
        )

        @pl.when(k == chunks - 1)
        def _():
            power_got[me_t] = power[...]
            for i in range(1, blocks):
                power_copy(i).start()

        def channel(c, carry):
            flat, turned = channel_rows(wide, c, stations, blocks, own, local)
            deep = 2 * blocks * per
            rows = pl.ds(pl.multiple_of(k * deep, deep), deep)
            both[c, rows, : stations * local] = flat
            both[c, rows, stations * local :] = turned
            return carry

        lax.fori_loop(0, own, channel, 0, unroll=4)
        return carry

    def power_copy(i):
        return pltpu.make_async_remote_copy(
            src_ref=power,
            dst_ref=power_got.at[me_t],
            send_sem=power_send.at[i],
            recv_sem=power_recv.at[i],
            device_id=(me_s, lax.rem(me_t + i, blocks)),
            device_id_type=MESH,
        )

    lax.fori_loop(0, chunks, arrange, 0)

    for i in range(1, blocks):
        power_copy(i).wait()
    powers[...] = power_got[...]

    def drain(job, carry):
        sent = spec.at[job, pl.ds(0, dests - 1)]
        pltpu.make_async_copy(sent, sent, spec_send.at[job]).wait()
        return carry

    lax.fori_loop(low, high, drain, 0)

    @pl.when(jnp.logical_not(first))
    def _():
        for k in range(chunks):
            halo(k, me_t - 1).wait_send()


def correlate_kernel(blocks, own, scale, group, both, powers, vis, power, out, out_sem):
    inputs = both.shape[2] // 2
    buffers = out.shape[0]

    def store(step):
        slot = lax.rem(step, buffers)
        return pltpu.make_async_copy(
            out.at[slot], vis.at[pl.ds(step * group, group)], out_sem.at[slot]
        )

    def products(step, carry):
        slot = lax.rem(step, buffers)
        pl.when(step >= buffers)(lambda: store(step - buffers).wait())
        for g in range(group):
            c = step * group + g
            prod = lax.dot_general(
                both[c, :, :inputs],
                both[c],
                (((0,), (0,)), ((), ())),
                preferred_element_type=jnp.float32,
            )
            out[slot, g, 0] = prod[:, :inputs] * scale
            out[slot, g, 1] = prod[:, inputs:] * scale
        store(step).start()
        return carry

    steps = own // group
    lax.fori_loop(0, steps, products, 0)

    me = lax.axis_index("tm")
    wide = powers.shape[2]
    row = lax.broadcasted_iota(jnp.int32, (wide, wide), 0)
    col = lax.broadcasted_iota(jnp.int32, (wide, wide), 1)
    total = jnp.zeros(power.shape, jnp.float32)
    for b in range(blocks):
        move = jnp.logical_and(row - me * own == col - b * own, col // own == b)
        total = total + lax.dot_general(
            powers[b],
            move.astype(jnp.float32),
            (((1,), (0,)), ((), ())),
            precision=lax.Precision.HIGHEST,
            preferred_element_type=jnp.float32,
        )
    power[...] = total * (1.0 / inputs)

    def drain(step, carry):
        store(step).wait()
        return carry

    lax.fori_loop(max(0, steps - buffers), steps, drain, 0)


def body(samples, history, taps):
    frames, local, frame_len = samples.shape
    span = taps.shape[0]
    stations, blocks = lax.axis_size("station"), lax.axis_size("tm")
    dests = stations * blocks
    inputs = stations * local
    own = frame_len // 2 // dests
    per = LANES // local
    chunks = frames // per
    depth = 2 * frames * blocks
    table = dft_table(stations, blocks, own, frame_len)
    hbm = pl.BlockSpec(memory_space=pltpu.HBM)
    vmem = pl.BlockSpec(memory_space=pltpu.VMEM)
    in_hbm = [pltpu.with_memory_space_constraint(x, pltpu.HBM) for x in (samples, history, taps)]
    both, powers = pl.pallas_call(
        functools.partial(spectra_kernel, stations, blocks, own, local, frames, span),
        in_specs=[hbm, hbm, hbm, hbm],
        out_specs=[vmem, vmem],
        out_shape=[
            jax.ShapeDtypeStruct((own, depth, 2 * inputs), jnp.bfloat16),
            jax.ShapeDtypeStruct((blocks, frames, blocks * own), jnp.float32),
        ],
        scratch_shapes=[
            pltpu.VMEM((span - 1 + 2 * frames, local, frame_len), jnp.bfloat16),
            pltpu.VMEM(taps.shape, jnp.float32),
            pltpu.VMEM(table.shape, jnp.bfloat16),
            pltpu.VMEM((LANES, frame_len), jnp.bfloat16),
            pltpu.VMEM((2 * chunks, dests, 2 * own, LANES), jnp.bfloat16),
            pltpu.VMEM((chunks, blocks, stations, 2 * own, LANES), jnp.bfloat16),
            pltpu.VMEM((stations, 2 * blocks * own, LANES), jnp.float32),
            pltpu.VMEM((frames, blocks * own), jnp.float32),
            pltpu.VMEM((blocks, frames, blocks * own), jnp.float32),
            pltpu.SemaphoreType.DMA((3,)),
            pltpu.SemaphoreType.DMA((blocks,)),
            pltpu.SemaphoreType.DMA((chunks,)),
            pltpu.SemaphoreType.DMA((chunks,)),
            pltpu.SemaphoreType.DMA((2 * chunks,)),
            pltpu.SemaphoreType.DMA((chunks,)),
            pltpu.SemaphoreType.DMA((blocks,)),
            pltpu.SemaphoreType.DMA((blocks,)),
        ],
        compiler_params=pltpu.CompilerParams(
            collective_id=0, has_side_effects=True, vmem_limit_bytes=VMEM_LIMIT
        ),
        cost_estimate=pl.CostEstimate(
            flops=8 * frames * local * frame_len * dests * own,
            bytes_accessed=8 * samples.size + table.size * 2,
            transcendentals=0,
        ),
    )(*in_hbm, table)

    group = math.gcd(own, 2)
    visibility, power = pl.pallas_call(
        functools.partial(correlate_kernel, blocks, own, 1.0 / (frames * blocks), group),
        in_specs=[vmem, vmem],
        out_specs=[pl.BlockSpec(memory_space=pl.ANY), vmem],
        out_shape=[
            jax.ShapeDtypeStruct((own, 2, inputs, inputs), jnp.float32),
            jax.ShapeDtypeStruct((frames, blocks * own), jnp.float32),
        ],
        scratch_shapes=[
            pltpu.VMEM((4, group, 2, inputs, inputs), jnp.float32),
            pltpu.SemaphoreType.DMA((4,)),
        ],
        compiler_params=pltpu.CompilerParams(vmem_limit_bytes=24 * 1024 * 1024),
    )(both, powers)
    return visibility, power


def solution(mesh):
    return jax.shard_map(
        body,
        mesh=mesh,
        in_specs=(P("tm", "station", None), P(None, "station", None), P()),
        out_specs=(P(("station", "tm"), None, None, None), P("tm", "station")),
        check_vma=False,
    )
```

```python
import functools
import math

import jax
import jax.numpy as jnp
import numpy as np
from jax import lax
from jax.experimental import pallas as pl
from jax.experimental.pallas import tpu as pltpu
from jax.sharding import PartitionSpec as P

MESH = pl.DeviceIdType.MESH
LANES = 128
VMEM_LIMIT = 44 * 1024 * 1024


def dft_table(stations, blocks, own, frame_len):
    channel = np.arange(stations * blocks * own).reshape(stations, blocks, own)
    channel = channel.transpose(1, 0, 2).reshape(-1)
    phase = channel[:, None] * np.arange(frame_len)[None, :] % frame_len
    angle = phase.astype(np.float32) * np.float32(2.0 * math.pi / frame_len)
    parts = np.stack([np.cos(angle), -np.sin(angle)], axis=0)
    parts = parts.reshape(2, blocks * stations, own, frame_len).transpose(1, 0, 2, 3)
    return jnp.asarray(parts.reshape(-1, frame_len).astype(jnp.bfloat16))


def channel_rows(wide, channel, stations, blocks, own, local):
    slots = LANES // local
    rows = 2 * blocks
    lane = lax.broadcasted_iota(jnp.int32, (rows, LANES), 1) // local
    sign = jnp.where(
        lax.broadcasted_iota(jnp.int32, (rows, stations * local), 0) < blocks, 1.0, -1.0
    )
    halves = []
    for h in range(stations // slots):
        parts = [
            wide[h * slots + s, pl.ds(channel, rows, stride=own), :] for s in range(slots)
        ]
        tiles = []
        for t in range(slots):
            tile = None
            for s in range(slots):
                shift = (s - t) % slots * local
                moved = parts[s] if shift == 0 else pltpu.roll(parts[s], shift, 1)
                tile = moved if tile is None else jnp.where(lane == s, moved, tile)
            tiles.append(tile)
        halves.append(tiles)
    flat, turned = [], []
    for t in range(slots):
        full = jnp.concatenate([half[t] for half in halves], axis=1)
        flat.append(full)
        turned.append(pltpu.roll(full, blocks, 0) * sign)
    flat = jnp.concatenate(flat, axis=0).astype(jnp.bfloat16)
    turned = jnp.concatenate(turned, axis=0).astype(jnp.bfloat16)
    return flat, turned


def spectra_kernel(
    stations, blocks, own, local, frames, span,
    samples, history, taps_hbm, table_hbm,
    both, powers, tail,
    ext, taps, table, weighted, spec, got, wide, power, power_got, tail_part, tail_out, tail_got,
    load_sem, table_sem, halo_send, halo_recv, spec_send, spec_recv, power_send, power_recv, tail_send, tail_recv,
):
    me_s, me_t = lax.axis_index("station"), lax.axis_index("tm")
    dests = stations * blocks
    per = LANES // local
    chunks = frames // per
    frame_len = samples.shape[2]
    hist = span - 1
    first = me_t == 0
    last = me_t == blocks - 1

    load_own = pltpu.make_async_copy(samples, ext.at[pl.ds(hist, frames)], load_sem.at[0])
    load_hist = pltpu.make_async_copy(history, ext.at[pl.ds(0, hist)], load_sem.at[1])

    load_taps = pltpu.make_async_copy(taps_hbm, taps, load_sem.at[2])

    depth = stations * 2 * own

    def load_table(plane):
        rows = pl.ds(pl.multiple_of(plane * depth, depth), depth)
        return pltpu.make_async_copy(table_hbm.at[rows], table.at[rows], table_sem.at[plane])

    load_own.start()
    pl.when(first)(load_hist.start)
    load_taps.start()

    @pl.when(jnp.logical_not(last))
    def _():
        for plane in reversed(range(blocks)):
            load_table(plane).start()

    barrier = pltpu.get_barrier_semaphore()

    def greet(i, carry):
        other = lax.rem(me_s * blocks + me_t + i, dests)
        pl.semaphore_signal(
            barrier,
            inc=1,
            device_id=(other // blocks, lax.rem(other, blocks)),
            device_id_type=MESH,
        )
        return carry

    lax.fori_loop(1, dests, greet, 0)
    load_own.wait()
    load_taps.wait()

    def filter_chunk(start):
        def tile(i, carry):
            lanes = pl.ds(pl.multiple_of(i * LANES, LANES), LANES)
            sums = [None] * per
            for e in range(per + span - 1):
                x = ext[start + e, :, lanes].astype(jnp.float32)
                for j in range(per):
                    tap = j + span - 1 - e
                    if 0 <= tap < span:
                        term = taps[tap : tap + 1, lanes] * x
                        sums[j] = term if sums[j] is None else sums[j] + term
            for j in range(per):
                weighted[j * local : (j + 1) * local, lanes] = sums[j].astype(jnp.bfloat16)
            return carry

        lax.fori_loop(0, frame_len // LANES, tile, 0)

    @pl.when(first)
    def _():
        load_hist.wait()
        filter_chunk(0)

    pl.semaphore_wait(barrier, dests - 1)

    def halo(k, target):
        return pltpu.make_async_remote_copy(
            src_ref=samples.at[pl.ds(k * per, per)],
            dst_ref=ext.at[pl.ds(hist + frames + k * per, per)],
            send_sem=halo_send.at[k],
            recv_sem=halo_recv.at[k],
            device_id=(me_s, target),
            device_id_type=MESH,
        )

    @pl.when(jnp.logical_not(first))
    def _():
        for k in range(chunks):
            halo(k, me_t - 1).start()

    def send(job, plane):
        k = lax.rem(job, chunks)
        block = jnp.where(job < chunks, 0, me_t + 1)

        def one(i, carry):
            s = lax.rem(me_s + i, stations)
            here = jnp.logical_and(i == 0, plane == me_t)
            piece = spec.at[job, plane * stations + s]

            @pl.when(here)
            def _():
                pltpu.make_async_copy(piece, got.at[k, block, me_s], spec_recv.at[k]).start()

            @pl.when(jnp.logical_not(here))
            def _():
                pltpu.make_async_remote_copy(
                    src_ref=piece,
                    dst_ref=got.at[k, block, me_s],
                    send_sem=spec_send.at[job],
                    recv_sem=spec_recv.at[k],
                    device_id=(s, plane),
                    device_id_type=MESH,
                ).start()

            return carry

        lax.fori_loop(0, stations, one, 0)

    low = jnp.where(first, 0, chunks)
    high = jnp.where(last, chunks, 2 * chunks)

    def tail_copy(which, i):
        s = lax.rem(me_s + i, stations)
        return pltpu.make_async_remote_copy(
            src_ref=tail_out.at[which, s],
            dst_ref=tail_got.at[me_s],
            send_sem=tail_send.at[which],
            recv_sem=tail_recv.at[0],
            device_id=(s, me_t + which),
            device_id_type=MESH,
        )

    above = blocks - 1 - me_t
    lane_frame = lax.broadcasted_iota(jnp.int32, tail_out.shape[2:3] + (LANES,), 1) // local
    pick_tail = (
        lane_frame == lax.broadcasted_iota(jnp.int32, lane_frame.shape, 0)
    ).astype(jnp.float32)

    def work(job, carry):
        @pl.when(job >= chunks)
        def _():
            halo(job - chunks, me_t).wait_recv()

        @pl.when(job == 2 * chunks - 1)
        def _():
            def older(old, carry):
                def plane_of(plane, carry):
                    send(old, plane)
                    return carry

                return lax.fori_loop(0, me_t, plane_of, carry)

            lax.fori_loop(chunks, 2 * chunks - 1, older, 0)

        pl.when(job > 0)(lambda: filter_chunk(job * per))

        def planes(i, carry):
            plane = jnp.where(i < above, blocks - 1 - i, jnp.where(i < blocks - 1, i - above, me_t))
            pl.when(job == low)(load_table(plane).wait)
            out = lax.dot_general(
                table[pl.ds(pl.multiple_of(plane * depth, depth), depth), :],
                weighted[...],
                (((1,), (1,)), ((), ())),
                preferred_element_type=jnp.float32,
            )
            out = out.astype(jnp.bfloat16).reshape(stations, 2 * own, LANES)
            spec[job, pl.ds(plane * stations, stations)] = out

            @pl.when(lax.rem(job, chunks) == chunks - 1)
            def _():
                values = out.astype(jnp.float32)
                values = values * values
                values = (values[:, :own] + values[:, own:]).reshape(stations * own, LANES)
                tail_part[plane] = lax.dot_general(
                    pick_tail,
                    values,
                    (((1,), (1,)), ((), ())),
                    precision=lax.Precision.HIGHEST,
                    preferred_element_type=jnp.float32,
                )

            near = jnp.logical_and(job < chunks - 1, plane == me_t + 1)
            now = jnp.where(job == 2 * chunks - 1, True, jnp.logical_and(plane >= me_t, jnp.logical_not(near)))
            pl.when(now)(lambda: send(job, plane))
            return carry

        lax.fori_loop(0, blocks, planes, 0)

        @pl.when(job == chunks - 1)
        def _():
            def near(old, carry):
                send(old, me_t + 1)
                return carry

            lax.fori_loop(0, chunks - 1, near, 0)

        @pl.when(lax.rem(job, chunks) == chunks - 1)
        def _():
            which = job // chunks
            for s in range(stations):
                tail_out[which, s] = jnp.concatenate(
                    [tail_part[plane, :, s * own : (s + 1) * own] for plane in range(blocks)],
                    axis=1,
                )

            @pl.when(which == 0)
            def _():
                pltpu.make_async_copy(
                    tail_out.at[0, me_s], tail_got.at[me_s], tail_recv.at[0]
                ).start()
                for i in range(1, stations):
                    tail_copy(0, i).start()

            @pl.when(which == 1)
            def _():
                for i in range(stations):
                    tail_copy(1, i).start()

        return carry

    lax.fori_loop(low, high, work, 0)

    power[...] = jnp.zeros_like(power)

    def arrange(k, carry):
        pltpu.make_async_copy(got.at[k], got.at[k], spec_recv.at[k]).wait()

        def fill(s, carry):
            for b in range(blocks):
                for p in range(2):
                    wide[s, (p * blocks + b) * own : (p * blocks + b + 1) * own, :] = got[
                        k, b, s, p * own : (p + 1) * own, :
                    ].astype(jnp.float32)
            return carry

        lax.fori_loop(0, stations, fill, 0)

        @pl.when(k < chunks - 1)
        def _():
            half = blocks * own
            total = jnp.zeros((half, LANES), jnp.float32)
            for s in range(stations):
                re, im = wide[s, :half, :], wide[s, half:, :]
                total = total + (re * re + im * im)
            frame = lax.broadcasted_iota(jnp.int32, (frames, LANES), 0) - k * per
            pick = (lax.broadcasted_iota(jnp.int32, (frames, LANES), 1) // local == frame).astype(
                jnp.float32
            )
            power[...] += lax.dot_general(
                pick,
                total,
                (((1,), (1,)), ((), ())),
                precision=lax.Precision.HIGHEST,
                preferred_element_type=jnp.float32,
            )

        @pl.when(k == chunks - 2)
        def _():
            power_got[me_t] = power[...]
            for i in range(1, blocks):
                power_copy(i).start()

        def channel(c, carry):
            flat, turned = channel_rows(wide, c, stations, blocks, own, local)
            deep = 2 * blocks * per
            rows = pl.ds(pl.multiple_of(k * deep, deep), deep)
            both[c, rows, : stations * local] = flat
            both[c, rows, stations * local :] = turned
            return carry

        lax.fori_loop(0, own, channel, 0, unroll=4)
        return carry

    def power_copy(i):
        return pltpu.make_async_remote_copy(
            src_ref=power,
            dst_ref=power_got.at[me_t],
            send_sem=power_send.at[i],
            recv_sem=power_recv.at[i],
            device_id=(me_s, lax.rem(me_t + i, blocks)),
            device_id_type=MESH,
        )

    lax.fori_loop(0, chunks, arrange, 0)

    for i in range(1, blocks):
        power_copy(i).wait()
    powers[...] = power_got[...]
    pltpu.make_async_copy(tail_got, tail_got, tail_recv.at[0]).wait()
    total = tail_got[0]
    for s in range(1, stations):
        total = total + tail_got[s]
    tail[...] = total

    @pl.when(first)
    def _():
        sent = tail_out.at[0, pl.ds(0, stations - 1)]
        pltpu.make_async_copy(sent, sent, tail_send.at[0]).wait()

    @pl.when(jnp.logical_not(last))
    def _():
        pltpu.make_async_copy(tail_out.at[1], tail_out.at[1], tail_send.at[1]).wait()

    def drain(job, carry):
        sent = spec.at[job, pl.ds(0, dests - 1)]
        pltpu.make_async_copy(sent, sent, spec_send.at[job]).wait()
        return carry

    lax.fori_loop(low, high, drain, 0)

    @pl.when(jnp.logical_not(first))
    def _():
        for k in range(chunks):
            halo(k, me_t - 1).wait_send()


def correlate_kernel(blocks, own, scale, group, per, both, powers, tail, vis, power, out, out_sem):
    inputs = both.shape[2] // 2
    buffers = out.shape[0]

    def store(step):
        slot = lax.rem(step, buffers)
        return pltpu.make_async_copy(
            out.at[slot], vis.at[pl.ds(step * group, group)], out_sem.at[slot]
        )

    def products(step, carry):
        slot = lax.rem(step, buffers)
        pl.when(step >= buffers)(lambda: store(step - buffers).wait())
        for g in range(group):
            c = step * group + g
            prod = lax.dot_general(
                both[c, :, :inputs],
                both[c],
                (((0,), (0,)), ((), ())),
                preferred_element_type=jnp.float32,
            )
            out[slot, g, 0] = prod[:, :inputs] * scale
            out[slot, g, 1] = prod[:, inputs:] * scale
        store(step).start()
        return carry

    steps = own // group
    lax.fori_loop(0, steps, products, 0)

    me = lax.axis_index("tm")
    wide = powers.shape[2]
    row = lax.broadcasted_iota(jnp.int32, (wide, wide), 0)
    col = lax.broadcasted_iota(jnp.int32, (wide, wide), 1)
    total = jnp.zeros(power.shape, jnp.float32)
    for b in range(blocks):
        move = jnp.logical_and(row - me * own == col - b * own, col // own == b)
        total = total + lax.dot_general(
            powers[b],
            move.astype(jnp.float32),
            (((1,), (0,)), ((), ())),
            precision=lax.Precision.HIGHEST,
            preferred_element_type=jnp.float32,
        )
    power[...] = total * (1.0 / inputs)
    power[power.shape[0] - per :, :] = tail[:per, :] * (1.0 / inputs)

    def drain(step, carry):
        store(step).wait()
        return carry

    lax.fori_loop(max(0, steps - buffers), steps, drain, 0)


def body(samples, history, taps):
    frames, local, frame_len = samples.shape
    span = taps.shape[0]
    stations, blocks = lax.axis_size("station"), lax.axis_size("tm")
    dests = stations * blocks
    inputs = stations * local
    own = frame_len // 2 // dests
    per = LANES // local
    chunks = frames // per
    depth = 2 * frames * blocks
    tail_rows = max(8, per)
    table = dft_table(stations, blocks, own, frame_len)
    hbm = pl.BlockSpec(memory_space=pltpu.HBM)
    vmem = pl.BlockSpec(memory_space=pltpu.VMEM)
    in_hbm = [pltpu.with_memory_space_constraint(x, pltpu.HBM) for x in (samples, history, taps)]
    both, powers, tail = pl.pallas_call(
        functools.partial(spectra_kernel, stations, blocks, own, local, frames, span),
        in_specs=[hbm, hbm, hbm, hbm],
        out_specs=[vmem, vmem, vmem],
        out_shape=[
            jax.ShapeDtypeStruct((own, depth, 2 * inputs), jnp.bfloat16),
            jax.ShapeDtypeStruct((blocks, frames, blocks * own), jnp.float32),
            jax.ShapeDtypeStruct((tail_rows, blocks * own), jnp.float32),
        ],
        scratch_shapes=[
            pltpu.VMEM((span - 1 + 2 * frames, local, frame_len), jnp.bfloat16),
            pltpu.VMEM(taps.shape, jnp.float32),
            pltpu.VMEM(table.shape, jnp.bfloat16),
            pltpu.VMEM((LANES, frame_len), jnp.bfloat16),
            pltpu.VMEM((2 * chunks, dests, 2 * own, LANES), jnp.bfloat16),
            pltpu.VMEM((chunks, blocks, stations, 2 * own, LANES), jnp.bfloat16),
            pltpu.VMEM((stations, 2 * blocks * own, LANES), jnp.float32),
            pltpu.VMEM((frames, blocks * own), jnp.float32),
            pltpu.VMEM((blocks, frames, blocks * own), jnp.float32),
            pltpu.VMEM((blocks, tail_rows, stations * own), jnp.float32),
            pltpu.VMEM((2, stations, tail_rows, blocks * own), jnp.float32),
            pltpu.VMEM((stations, tail_rows, blocks * own), jnp.float32),
            pltpu.SemaphoreType.DMA((3,)),
            pltpu.SemaphoreType.DMA((blocks,)),
            pltpu.SemaphoreType.DMA((chunks,)),
            pltpu.SemaphoreType.DMA((chunks,)),
            pltpu.SemaphoreType.DMA((2 * chunks,)),
            pltpu.SemaphoreType.DMA((chunks,)),
            pltpu.SemaphoreType.DMA((blocks,)),
            pltpu.SemaphoreType.DMA((blocks,)),
            pltpu.SemaphoreType.DMA((2,)),
            pltpu.SemaphoreType.DMA((1,)),
        ],
        compiler_params=pltpu.CompilerParams(
            collective_id=0, has_side_effects=True, vmem_limit_bytes=VMEM_LIMIT
        ),
        cost_estimate=pl.CostEstimate(
            flops=8 * frames * local * frame_len * dests * own,
            bytes_accessed=8 * samples.size + table.size * 2,
            transcendentals=0,
        ),
    )(*in_hbm, table)

    group = math.gcd(own, 2)
    visibility, power = pl.pallas_call(
        functools.partial(correlate_kernel, blocks, own, 1.0 / (frames * blocks), group, per),
        in_specs=[vmem, vmem, vmem],
        out_specs=[pl.BlockSpec(memory_space=pl.ANY), vmem],
        out_shape=[
            jax.ShapeDtypeStruct((own, 2, inputs, inputs), jnp.float32),
            jax.ShapeDtypeStruct((frames, blocks * own), jnp.float32),
        ],
        scratch_shapes=[
            pltpu.VMEM((4, group, 2, inputs, inputs), jnp.float32),
            pltpu.SemaphoreType.DMA((4,)),
        ],
        compiler_params=pltpu.CompilerParams(vmem_limit_bytes=24 * 1024 * 1024),
    )(both, powers, tail)
    return visibility, power


def solution(mesh):
    return jax.shard_map(
        body,
        mesh=mesh,
        in_specs=(P("tm", "station", None), P(None, "station", None), P()),
        out_specs=(P(("station", "tm"), None, None, None), P("tm", "station")),
        check_vma=False,
    )
```

```python
import functools
import math

import jax
import jax.numpy as jnp
import numpy as np
from jax import lax
from jax.experimental import pallas as pl
from jax.experimental.pallas import tpu as pltpu
from jax.sharding import PartitionSpec as P

MESH = pl.DeviceIdType.MESH
LANES = 128
VMEM_LIMIT = 44 * 1024 * 1024


def halves_of(own):
    return 2 if own % 32 == 0 else 1


def dft_table(stations, blocks, own, frame_len):
    channel = np.arange(stations * blocks * own).reshape(stations, blocks, own)
    channel = channel.transpose(1, 0, 2).reshape(-1)
    phase = channel[:, None] * np.arange(frame_len)[None, :] % frame_len
    angle = phase.astype(np.float32) * np.float32(2.0 * math.pi / frame_len)
    parts = np.stack([np.cos(angle), -np.sin(angle)], axis=0)
    halves = halves_of(own)
    parts = parts.reshape(2, blocks * stations, halves, own // halves, frame_len)
    parts = parts.transpose(1, 2, 0, 3, 4)
    return jnp.asarray(parts.reshape(-1, frame_len).astype(jnp.bfloat16))


def channel_rows(wide, channel, stations, blocks, own, local):
    slots = LANES // local
    rows = 2 * blocks
    lane = lax.broadcasted_iota(jnp.int32, (rows, LANES), 1) // local
    sign = jnp.where(
        lax.broadcasted_iota(jnp.int32, (rows, stations * local), 0) < blocks, 1.0, -1.0
    )
    halves = []
    for h in range(stations // slots):
        parts = [
            wide[h * slots + s, pl.ds(channel, rows, stride=own), :] for s in range(slots)
        ]
        tiles = []
        for t in range(slots):
            tile = None
            for s in range(slots):
                shift = (s - t) % slots * local
                moved = parts[s] if shift == 0 else pltpu.roll(parts[s], shift, 1)
                tile = moved if tile is None else jnp.where(lane == s, moved, tile)
            tiles.append(tile)
        halves.append(tiles)
    flat, turned = [], []
    for t in range(slots):
        full = jnp.concatenate([half[t] for half in halves], axis=1)
        flat.append(full)
        turned.append(pltpu.roll(full, blocks, 0) * sign)
    flat = jnp.concatenate(flat, axis=0).astype(jnp.bfloat16)
    turned = jnp.concatenate(turned, axis=0).astype(jnp.bfloat16)
    return flat, turned


def spectra_kernel(
    stations, blocks, own, local, frames, span,
    samples, history, taps_hbm, table_hbm,
    both, powers, tail,
    ext, taps, table, weighted, spec, got, wide, power, power_got, tail_part, tail_out, tail_got, tail_next, tail_own,
    load_sem, table_sem, halo_send, halo_recv, spec_send, spec_recv, power_send, power_recv, tail_send, tail_recv,
):
    me_s, me_t = lax.axis_index("station"), lax.axis_index("tm")
    dests = stations * blocks
    halves = halves_of(own)
    sub = own // halves
    per = LANES // local
    chunks = frames // per
    frame_len = samples.shape[2]
    hist = span - 1
    first = me_t == 0
    last = me_t == blocks - 1

    load_own = pltpu.make_async_copy(samples, ext.at[pl.ds(hist, frames)], load_sem.at[0])
    load_hist = pltpu.make_async_copy(history, ext.at[pl.ds(0, hist)], load_sem.at[1])

    load_taps = pltpu.make_async_copy(taps_hbm, taps, load_sem.at[2])

    depth = stations * 2 * own

    def load_table(plane):
        rows = pl.ds(pl.multiple_of(plane * depth, depth), depth)
        return pltpu.make_async_copy(table_hbm.at[rows], table.at[rows], table_sem.at[plane])

    load_own.start()
    pl.when(first)(load_hist.start)
    load_taps.start()

    @pl.when(jnp.logical_not(last))
    def _():
        for plane in reversed(range(blocks)):
            load_table(plane).start()

    barrier = pltpu.get_barrier_semaphore()

    def greet(i, carry):
        other = lax.rem(me_s * blocks + me_t + i, dests)
        pl.semaphore_signal(
            barrier,
            inc=1,
            device_id=(other // blocks, lax.rem(other, blocks)),
            device_id_type=MESH,
        )
        return carry

    lax.fori_loop(1, dests, greet, 0)
    load_own.wait()
    load_taps.wait()

    def filter_chunk(start):
        def tile(i, carry):
            lanes = pl.ds(pl.multiple_of(i * LANES, LANES), LANES)
            sums = [None] * per
            for e in range(per + span - 1):
                x = ext[start + e, :, lanes].astype(jnp.float32)
                for j in range(per):
                    tap = j + span - 1 - e
                    if 0 <= tap < span:
                        term = taps[tap : tap + 1, lanes] * x
                        sums[j] = term if sums[j] is None else sums[j] + term
            for j in range(per):
                weighted[j * local : (j + 1) * local, lanes] = sums[j].astype(jnp.bfloat16)
            return carry

        lax.fori_loop(0, frame_len // LANES, tile, 0)

    @pl.when(first)
    def _():
        load_hist.wait()
        filter_chunk(0)

    pl.semaphore_wait(barrier, dests - 1)

    def halo(k, target):
        return pltpu.make_async_remote_copy(
            src_ref=samples.at[pl.ds(k * per, per)],
            dst_ref=ext.at[pl.ds(hist + frames + k * per, per)],
            send_sem=halo_send.at[k],
            recv_sem=halo_recv.at[k],
            device_id=(me_s, target),
            device_id_type=MESH,
        )

    @pl.when(jnp.logical_not(first))
    def _():
        for k in range(chunks):
            halo(k, me_t - 1).start()

    def send(job, plane, half=None):
        k = lax.rem(job, chunks)
        rows = pl.ds(0, 2 * own) if half is None else pl.ds(half * 2 * sub, 2 * sub)
        landed = spec_recv.at[k if half is None else k + half]
        block = jnp.where(job < chunks, 0, me_t + 1)

        def one(i, carry):
            s = lax.rem(me_s + i, stations)
            here = jnp.logical_and(i == 0, plane == me_t)
            piece = spec.at[job, plane * stations + s, rows]
            place = got.at[k, block, me_s, rows]

            @pl.when(here)
            def _():
                pltpu.make_async_copy(piece, place, landed).start()

            @pl.when(jnp.logical_not(here))
            def _():
                pltpu.make_async_remote_copy(
                    src_ref=piece,
                    dst_ref=place,
                    send_sem=spec_send.at[job],
                    recv_sem=landed,
                    device_id=(s, plane),
                    device_id_type=MESH,
                ).start()

            return carry

        lax.fori_loop(0, stations, one, 0)

    low = jnp.where(first, 0, chunks)
    high = jnp.where(last, chunks, 2 * chunks)

    def tail_copy(which, i):
        s = lax.rem(me_s + i, stations)
        return pltpu.make_async_remote_copy(
            src_ref=tail_out.at[which, s],
            dst_ref=tail_got.at[which, me_s],
            send_sem=tail_send.at[which],
            recv_sem=tail_recv.at[which],
            device_id=(s, me_t),
            device_id_type=MESH,
        )

    above = blocks - 1 - me_t
    lane_frame = lax.broadcasted_iota(jnp.int32, tail_out.shape[2:3] + (LANES,), 1) // local
    pick_tail = (
        lane_frame == lax.broadcasted_iota(jnp.int32, lane_frame.shape, 0)
    ).astype(jnp.float32)

    def work(job, carry):
        @pl.when(job >= chunks)
        def _():
            halo(job - chunks, me_t).wait_recv()

        @pl.when(job == 2 * chunks - 1)
        def _():
            def older(old, carry):
                def plane_of(plane, carry):
                    send(old, plane)
                    return carry

                return lax.fori_loop(0, me_t, plane_of, carry)

            lax.fori_loop(chunks, 2 * chunks - 1, older, 0)

        pl.when(job > 0)(lambda: filter_chunk(job * per))

        closing = lax.rem(job, chunks) == chunks - 1

        def plane_of(i):
            return jnp.where(i < above, blocks - 1 - i, jnp.where(i < blocks - 1, i - above, me_t))

        def planes(i, carry):
            plane = plane_of(i)
            pl.when(job == low)(load_table(plane).wait)
            out = lax.dot_general(
                table[pl.ds(pl.multiple_of(plane * depth, depth), depth), :],
                weighted[...],
                (((1,), (1,)), ((), ())),
                preferred_element_type=jnp.float32,
            )
            out = out.astype(jnp.bfloat16).reshape(stations, 2 * own, LANES)
            spec[job, pl.ds(plane * stations, stations)] = out

            @pl.when(closing)
            def _():
                values = out.astype(jnp.float32)
                values = values * values
                values = values.reshape(stations * halves, 2 * sub, LANES)
                values = (values[:, :sub] + values[:, sub:]).reshape(stations * own, LANES)
                tail_part[plane] = lax.dot_general(
                    pick_tail,
                    values,
                    (((1,), (1,)), ((), ())),
                    precision=lax.Precision.HIGHEST,
                    preferred_element_type=jnp.float32,
                )

            near = jnp.logical_and(job < chunks - 1, plane == me_t + 1)
            now = jnp.logical_and(plane >= me_t, jnp.logical_not(near))
            pl.when(jnp.logical_and(now, jnp.logical_not(closing)))(lambda: send(job, plane))

            @pl.when(job == chunks - 1)
            def _():
                for half in range(halves):
                    send(job, plane, half)

            return carry

        lax.fori_loop(0, blocks, planes, 0)

        @pl.when(job == 2 * chunks - 1)
        def _():
            for half in range(halves):

                def finish(i, carry):
                    send(job, plane_of(i), half)
                    return carry

                lax.fori_loop(0, blocks, finish, 0)

        @pl.when(job == chunks - 1)
        def _():
            def near(old, carry):
                send(old, me_t + 1)
                return carry

            lax.fori_loop(0, chunks - 1, near, 0)

        @pl.when(lax.rem(job, chunks) == chunks - 1)
        def _():
            which = job // chunks
            for s in range(stations):
                tail_out[which, s] = jnp.concatenate(
                    [tail_part[plane, :, s * own : (s + 1) * own] for plane in range(blocks)],
                    axis=1,
                )

            pltpu.make_async_copy(
                tail_out.at[which, me_s], tail_got.at[which, me_s], tail_recv.at[which]
            ).start()
            for i in range(1, stations):
                tail_copy(which, i).start()

        return carry

    lax.fori_loop(low, high, work, 0)

    power[...] = jnp.zeros_like(power)

    def fill(k, half):
        def one(s, carry):
            for b in range(blocks):
                for p in range(2):
                    base = (p * blocks + b) * own + half * sub
                    rows = (half * 2 + p) * sub
                    wide[s, base : base + sub, :] = got[k, b, s, rows : rows + sub, :].astype(
                        jnp.float32
                    )
            return carry

        lax.fori_loop(0, stations, one, 0)

    def channels(k, start, stop):
        deep = 2 * blocks * per
        rows = pl.ds(k * deep if isinstance(k, int) else pl.multiple_of(k * deep, deep), deep)

        def channel(c, carry):
            flat, turned = channel_rows(wide, c, stations, blocks, own, local)
            both[c, rows, : stations * local] = flat
            both[c, rows, stations * local :] = turned
            return carry

        lax.fori_loop(start, stop, channel, 0, unroll=8)

    def arrange(k, carry):
        pltpu.make_async_copy(got.at[k], got.at[k], spec_recv.at[k]).wait()

        for half in range(halves):
            fill(k, half)

        half = blocks * own
        total = jnp.zeros((half, LANES), jnp.float32)
        for s in range(stations):
            re, im = wide[s, :half, :], wide[s, half:, :]
            total = total + (re * re + im * im)
        frame = lax.broadcasted_iota(jnp.int32, (frames, LANES), 0) - k * per
        pick = (lax.broadcasted_iota(jnp.int32, (frames, LANES), 1) // local == frame).astype(
            jnp.float32
        )
        power[...] += lax.dot_general(
            pick,
            total,
            (((1,), (1,)), ((), ())),
            precision=lax.Precision.HIGHEST,
            preferred_element_type=jnp.float32,
        )

        @pl.when(k == chunks - 2)
        def _():
            power_got[me_t] = power[...]
            for i in range(1, blocks):
                power_copy(i).start()

        channels(k, 0, own)
        return carry

    def power_copy(i):
        return pltpu.make_async_remote_copy(
            src_ref=power,
            dst_ref=power_got.at[me_t],
            send_sem=power_send.at[i],
            recv_sem=power_recv.at[i],
            device_id=(me_s, lax.rem(me_t + i, blocks)),
            device_id_type=MESH,
        )

    def tail_sum(which):
        pltpu.make_async_copy(tail_got.at[which], tail_got.at[which], tail_recv.at[which]).wait()
        total = tail_got[which, 0]
        for s in range(1, stations):
            total = total + tail_got[which, s]
        return total

    def tail_forward(target):
        return pltpu.make_async_remote_copy(
            src_ref=tail_next,
            dst_ref=tail_own,
            send_sem=tail_send.at[2],
            recv_sem=tail_recv.at[2],
            device_id=(me_s, target),
            device_id_type=MESH,
        )

    @pl.when(jnp.logical_not(last))
    def _():
        tail_next[...] = tail_sum(1)
        tail_forward(me_t + 1).start()

    lax.fori_loop(0, chunks - 1, arrange, 0)
    for half in range(halves):
        part = got.at[chunks - 1, :, :, pl.ds(half * 2 * sub, 2 * sub)]
        pltpu.make_async_copy(part, part, spec_recv.at[chunks - 1 + half]).wait()
        fill(chunks - 1, half)
        channels(chunks - 1, half * sub, (half + 1) * sub)

    for i in range(1, blocks):
        power_copy(i).wait()
    powers[...] = power_got[...]

    def tail_drain(which):
        sent = tail_out.at[which, pl.ds(0, stations - 1)]
        pltpu.make_async_copy(sent, sent, tail_send.at[which]).wait()

    @pl.when(first)
    def _():
        tail[...] = tail_sum(0)
        tail_drain(0)

    @pl.when(jnp.logical_not(first))
    def _():
        tail_forward(me_t).wait_recv()
        tail[...] = tail_own[...]

    @pl.when(jnp.logical_not(last))
    def _():
        tail_drain(1)
        tail_forward(me_t + 1).wait_send()

    def drain(job, carry):
        sent = spec.at[job, pl.ds(0, dests - 1)]
        pltpu.make_async_copy(sent, sent, spec_send.at[job]).wait()
        return carry

    lax.fori_loop(low, high, drain, 0)

    @pl.when(jnp.logical_not(first))
    def _():
        for k in range(chunks):
            halo(k, me_t - 1).wait_send()


def correlate_kernel(blocks, own, scale, group, per, both, powers, tail, vis, power, out, out_sem):
    inputs = both.shape[2] // 2
    buffers = out.shape[0]

    def store(step):
        slot = lax.rem(step, buffers)
        return pltpu.make_async_copy(
            out.at[slot], vis.at[pl.ds(step * group, group)], out_sem.at[slot]
        )

    def products(step, carry):
        slot = lax.rem(step, buffers)
        pl.when(step >= buffers)(lambda: store(step - buffers).wait())
        for g in range(group):
            c = step * group + g
            prod = lax.dot_general(
                both[c, :, :inputs],
                both[c],
                (((0,), (0,)), ((), ())),
                preferred_element_type=jnp.float32,
            )
            out[slot, g, 0] = prod[:, :inputs] * scale
            out[slot, g, 1] = prod[:, inputs:] * scale
        store(step).start()
        return carry

    steps = own // group
    lax.fori_loop(0, steps, products, 0)

    me = lax.axis_index("tm")
    wide = powers.shape[2]
    row = lax.broadcasted_iota(jnp.int32, (wide, wide), 0)
    col = lax.broadcasted_iota(jnp.int32, (wide, wide), 1)
    total = jnp.zeros(power.shape, jnp.float32)
    for b in range(blocks):
        move = jnp.logical_and(row - me * own == col - b * own, col // own == b)
        total = total + lax.dot_general(
            powers[b],
            move.astype(jnp.float32),
            (((1,), (0,)), ((), ())),
            precision=lax.Precision.HIGHEST,
            preferred_element_type=jnp.float32,
        )
    power[...] = total * (1.0 / inputs)
    power[power.shape[0] - per :, :] = tail[:per, :] * (1.0 / inputs)

    def drain(step, carry):
        store(step).wait()
        return carry

    lax.fori_loop(max(0, steps - buffers), steps, drain, 0)


def body(samples, history, taps):
    frames, local, frame_len = samples.shape
    span = taps.shape[0]
    stations, blocks = lax.axis_size("station"), lax.axis_size("tm")
    dests = stations * blocks
    inputs = stations * local
    own = frame_len // 2 // dests
    per = LANES // local
    chunks = frames // per
    depth = 2 * frames * blocks
    tail_rows = max(8, per)
    table = dft_table(stations, blocks, own, frame_len)
    hbm = pl.BlockSpec(memory_space=pltpu.HBM)
    vmem = pl.BlockSpec(memory_space=pltpu.VMEM)
    in_hbm = [pltpu.with_memory_space_constraint(x, pltpu.HBM) for x in (samples, history, taps)]
    both, powers, tail = pl.pallas_call(
        functools.partial(spectra_kernel, stations, blocks, own, local, frames, span),
        in_specs=[hbm, hbm, hbm, hbm],
        out_specs=[vmem, vmem, vmem],
        out_shape=[
            jax.ShapeDtypeStruct((own, depth, 2 * inputs), jnp.bfloat16),
            jax.ShapeDtypeStruct((blocks, frames, blocks * own), jnp.float32),
            jax.ShapeDtypeStruct((tail_rows, blocks * own), jnp.float32),
        ],
        scratch_shapes=[
            pltpu.VMEM((span - 1 + 2 * frames, local, frame_len), jnp.bfloat16),
            pltpu.VMEM(taps.shape, jnp.float32),
            pltpu.VMEM(table.shape, jnp.bfloat16),
            pltpu.VMEM((LANES, frame_len), jnp.bfloat16),
            pltpu.VMEM((2 * chunks, dests, 2 * own, LANES), jnp.bfloat16),
            pltpu.VMEM((chunks, blocks, stations, 2 * own, LANES), jnp.bfloat16),
            pltpu.VMEM((stations, 2 * blocks * own, LANES), jnp.float32),
            pltpu.VMEM((frames, blocks * own), jnp.float32),
            pltpu.VMEM((blocks, frames, blocks * own), jnp.float32),
            pltpu.VMEM((blocks, tail_rows, stations * own), jnp.float32),
            pltpu.VMEM((2, stations, tail_rows, blocks * own), jnp.float32),
            pltpu.VMEM((2, stations, tail_rows, blocks * own), jnp.float32),
            pltpu.VMEM((tail_rows, blocks * own), jnp.float32),
            pltpu.VMEM((tail_rows, blocks * own), jnp.float32),
            pltpu.SemaphoreType.DMA((3,)),
            pltpu.SemaphoreType.DMA((blocks,)),
            pltpu.SemaphoreType.DMA((chunks,)),
            pltpu.SemaphoreType.DMA((chunks,)),
            pltpu.SemaphoreType.DMA((2 * chunks,)),
            pltpu.SemaphoreType.DMA((chunks - 1 + halves_of(own),)),
            pltpu.SemaphoreType.DMA((blocks,)),
            pltpu.SemaphoreType.DMA((blocks,)),
            pltpu.SemaphoreType.DMA((3,)),
            pltpu.SemaphoreType.DMA((3,)),
        ],
        compiler_params=pltpu.CompilerParams(
            collective_id=0, has_side_effects=True, vmem_limit_bytes=VMEM_LIMIT
        ),
        cost_estimate=pl.CostEstimate(
            flops=8 * frames * local * frame_len * dests * own,
            bytes_accessed=8 * samples.size + table.size * 2,
            transcendentals=0,
        ),
    )(*in_hbm, table)

    group = math.gcd(own, 2)
    visibility, power = pl.pallas_call(
        functools.partial(correlate_kernel, blocks, own, 1.0 / (frames * blocks), group, per),
        in_specs=[vmem, vmem, vmem],
        out_specs=[pl.BlockSpec(memory_space=pl.ANY), vmem],
        out_shape=[
            jax.ShapeDtypeStruct((own, 2, inputs, inputs), jnp.float32),
            jax.ShapeDtypeStruct((frames, blocks * own), jnp.float32),
        ],
        scratch_shapes=[
            pltpu.VMEM((4, group, 2, inputs, inputs), jnp.float32),
            pltpu.SemaphoreType.DMA((4,)),
        ],
        compiler_params=pltpu.CompilerParams(vmem_limit_bytes=24 * 1024 * 1024),
    )(both, powers, tail)
    return visibility, power


def solution(mesh):
    return jax.shard_map(
        body,
        mesh=mesh,
        in_specs=(P("tm", "station", None), P(None, "station", None), P()),
        out_specs=(P(("station", "tm"), None, None, None), P("tm", "station")),
        check_vma=False,
    )
```

```python
import functools
import math

import jax
import jax.numpy as jnp
import numpy as np
from jax import lax
from jax.experimental import pallas as pl
from jax.experimental.pallas import tpu as pltpu
from jax.sharding import PartitionSpec as P

MESH = pl.DeviceIdType.MESH
LANES = 128
VMEM_LIMIT = 44 * 1024 * 1024


def halves_of(own):
    return 2 if own % 32 == 0 else 1


def dft_table(stations, blocks, own, frame_len):
    channel = np.arange(stations * blocks * own).reshape(stations, blocks, own)
    channel = channel.transpose(1, 0, 2).reshape(-1)
    phase = channel[:, None] * np.arange(frame_len)[None, :] % frame_len
    angle = phase.astype(np.float32) * np.float32(2.0 * math.pi / frame_len)
    parts = np.stack([np.cos(angle), -np.sin(angle)], axis=0)
    halves = halves_of(own)
    parts = parts.reshape(2, blocks * stations, halves, own // halves, frame_len)
    parts = parts.transpose(1, 2, 0, 3, 4)
    return jnp.asarray(parts.reshape(-1, frame_len).astype(jnp.bfloat16))


def channel_rows(wide, channel, stations, blocks, own, local):
    slots = LANES // local
    rows = 2 * blocks
    lane = lax.broadcasted_iota(jnp.int32, (rows, LANES), 1) // local
    sign = jnp.where(
        lax.broadcasted_iota(jnp.int32, (rows, stations * local), 0) < blocks, 1.0, -1.0
    )
    halves = []
    for h in range(stations // slots):
        parts = [
            wide[h * slots + s, pl.ds(channel, rows, stride=own), :] for s in range(slots)
        ]
        tiles = []
        for t in range(slots):
            tile = None
            for s in range(slots):
                shift = (s - t) % slots * local
                moved = parts[s] if shift == 0 else pltpu.roll(parts[s], shift, 1)
                tile = moved if tile is None else jnp.where(lane == s, moved, tile)
            tiles.append(tile)
        halves.append(tiles)
    flat, turned = [], []
    for t in range(slots):
        full = jnp.concatenate([half[t] for half in halves], axis=1)
        flat.append(full)
        turned.append(pltpu.roll(full, blocks, 0) * sign)
    flat = jnp.concatenate(flat, axis=0).astype(jnp.bfloat16)
    turned = jnp.concatenate(turned, axis=0).astype(jnp.bfloat16)
    return flat, turned


def spectra_kernel(
    stations, blocks, own, local, frames, span,
    samples, history, taps_hbm, table_hbm,
    both, powers, tail,
    ext, taps, table, weighted, spec, got, wide, power, power_got, tail_part, tail_out, tail_got, tail_next, tail_own,
    load_sem, table_sem, halo_send, halo_recv, spec_send, spec_recv, power_send, power_recv, tail_send, tail_recv,
):
    me_s, me_t = lax.axis_index("station"), lax.axis_index("tm")
    dests = stations * blocks
    halves = halves_of(own)
    sub = own // halves
    per = LANES // local
    chunks = frames // per
    frame_len = samples.shape[2]
    hist = span - 1
    first = me_t == 0
    last = me_t == blocks - 1

    load_own = pltpu.make_async_copy(samples, ext.at[pl.ds(hist, frames)], load_sem.at[0])
    load_hist = pltpu.make_async_copy(history, ext.at[pl.ds(0, hist)], load_sem.at[1])

    load_taps = pltpu.make_async_copy(taps_hbm, taps, load_sem.at[2])

    depth = stations * 2 * own

    def load_table(plane):
        rows = pl.ds(pl.multiple_of(plane * depth, depth), depth)
        return pltpu.make_async_copy(table_hbm.at[rows], table.at[rows], table_sem.at[plane])

    load_own.start()
    pl.when(first)(load_hist.start)
    load_taps.start()

    @pl.when(jnp.logical_not(last))
    def _():
        for plane in reversed(range(blocks)):
            load_table(plane).start()

    barrier = pltpu.get_barrier_semaphore()

    def greet(i, carry):
        other = lax.rem(me_s * blocks + me_t + i, dests)
        pl.semaphore_signal(
            barrier,
            inc=1,
            device_id=(other // blocks, lax.rem(other, blocks)),
            device_id_type=MESH,
        )
        return carry

    lax.fori_loop(1, dests, greet, 0)
    load_own.wait()
    load_taps.wait()

    def filter_chunk(start):
        def tile(i, carry):
            lanes = pl.ds(pl.multiple_of(i * LANES, LANES), LANES)
            sums = [None] * per
            for e in range(per + span - 1):
                x = ext[start + e, :, lanes].astype(jnp.float32)
                for j in range(per):
                    tap = j + span - 1 - e
                    if 0 <= tap < span:
                        term = taps[tap : tap + 1, lanes] * x
                        sums[j] = term if sums[j] is None else sums[j] + term
            for j in range(per):
                weighted[j * local : (j + 1) * local, lanes] = sums[j].astype(jnp.bfloat16)
            return carry

        lax.fori_loop(0, frame_len // LANES, tile, 0)

    @pl.when(first)
    def _():
        load_hist.wait()
        filter_chunk(0)

    pl.semaphore_wait(barrier, dests - 1)

    def halo(k, target):
        return pltpu.make_async_remote_copy(
            src_ref=samples.at[pl.ds(k * per, per)],
            dst_ref=ext.at[pl.ds(hist + frames + k * per, per)],
            send_sem=halo_send.at[k],
            recv_sem=halo_recv.at[k],
            device_id=(me_s, target),
            device_id_type=MESH,
        )

    @pl.when(jnp.logical_not(first))
    def _():
        for k in range(chunks):
            halo(k, me_t - 1).start()

    def send(job, plane, half=None):
        k = lax.rem(job, chunks)
        rows = pl.ds(0, 2 * own) if half is None else pl.ds(half * 2 * sub, 2 * sub)
        landed = spec_recv.at[k if half is None else k + half]
        block = jnp.where(job < chunks, 0, me_t + 1)

        def one(i, carry):
            s = lax.rem(me_s + i, stations)
            here = jnp.logical_and(i == 0, plane == me_t)
            piece = spec.at[job, plane * stations + s, rows]
            place = got.at[k, block, me_s, rows]

            @pl.when(here)
            def _():
                pltpu.make_async_copy(piece, place, landed).start()

            @pl.when(jnp.logical_not(here))
            def _():
                pltpu.make_async_remote_copy(
                    src_ref=piece,
                    dst_ref=place,
                    send_sem=spec_send.at[job],
                    recv_sem=landed,
                    device_id=(s, plane),
                    device_id_type=MESH,
                ).start()

            return carry

        lax.fori_loop(0, stations, one, 0)

    low = jnp.where(first, 0, chunks)
    high = jnp.where(last, chunks, 2 * chunks)

    def tail_copy(which, i):
        s = lax.rem(me_s + i, stations)
        return pltpu.make_async_remote_copy(
            src_ref=tail_out.at[which, s],
            dst_ref=tail_got.at[which, me_s],
            send_sem=tail_send.at[which],
            recv_sem=tail_recv.at[which],
            device_id=(s, me_t),
            device_id_type=MESH,
        )

    above = blocks - 1 - me_t
    lane_frame = lax.broadcasted_iota(jnp.int32, tail_out.shape[2:3] + (LANES,), 1) // local
    pick_tail = (
        lane_frame == lax.broadcasted_iota(jnp.int32, lane_frame.shape, 0)
    ).astype(jnp.float32)

    def work(job, carry):
        @pl.when(job >= chunks)
        def _():
            halo(job - chunks, me_t).wait_recv()

        pl.when(job > 0)(lambda: filter_chunk(job * per))

        closing = lax.rem(job, chunks) == chunks - 1

        def plane_of(i):
            return jnp.where(i < above, blocks - 1 - i, jnp.where(i < blocks - 1, i - above, me_t))

        def planes(i, carry):
            plane = plane_of(i)
            pl.when(job == low)(load_table(plane).wait)
            out = lax.dot_general(
                table[pl.ds(pl.multiple_of(plane * depth, depth), depth), :],
                weighted[...],
                (((1,), (1,)), ((), ())),
                preferred_element_type=jnp.float32,
            )
            out = out.astype(jnp.bfloat16).reshape(stations, 2 * own, LANES)
            spec[job, pl.ds(plane * stations, stations)] = out

            @pl.when(closing)
            def _():
                values = out.astype(jnp.float32)
                values = values * values
                values = values.reshape(stations * halves, 2 * sub, LANES)
                values = (values[:, :sub] + values[:, sub:]).reshape(stations * own, LANES)
                tail_part[plane] = lax.dot_general(
                    pick_tail,
                    values,
                    (((1,), (1,)), ((), ())),
                    precision=lax.Precision.HIGHEST,
                    preferred_element_type=jnp.float32,
                )

            near = jnp.logical_and(job < chunks - 1, plane == me_t + 1)
            now = jnp.logical_and(plane >= me_t, jnp.logical_not(near))
            pl.when(jnp.logical_and(now, jnp.logical_not(closing)))(lambda: send(job, plane))

            @pl.when(job == chunks - 1)
            def _():
                for half in range(halves):
                    send(job, plane, half)

            return carry

        lax.fori_loop(0, blocks, planes, 0)

        @pl.when(job == 2 * chunks - 2)
        def _():
            def older(old, carry):
                def plane_of(plane, carry):
                    send(old, plane)
                    return carry

                return lax.fori_loop(0, me_t, plane_of, carry)

            lax.fori_loop(chunks, 2 * chunks - 1, older, 0)

        @pl.when(job == 2 * chunks - 1)
        def _():
            for half in range(halves):

                def finish(i, carry):
                    send(job, plane_of(i), half)
                    return carry

                lax.fori_loop(0, blocks, finish, 0)

        @pl.when(job == chunks - 1)
        def _():
            def near(old, carry):
                send(old, me_t + 1)
                return carry

            lax.fori_loop(0, chunks - 1, near, 0)

        @pl.when(lax.rem(job, chunks) == chunks - 1)
        def _():
            which = job // chunks
            for s in range(stations):
                tail_out[which, s] = jnp.concatenate(
                    [tail_part[plane, :, s * own : (s + 1) * own] for plane in range(blocks)],
                    axis=1,
                )

            pltpu.make_async_copy(
                tail_out.at[which, me_s], tail_got.at[which, me_s], tail_recv.at[which]
            ).start()
            for i in range(1, stations):
                tail_copy(which, i).start()

        return carry

    lax.fori_loop(low, high, work, 0)

    power[...] = jnp.zeros_like(power)

    def fill(k, half):
        def one(s, carry):
            for b in range(blocks):
                for p in range(2):
                    base = (p * blocks + b) * own + half * sub
                    rows = (half * 2 + p) * sub
                    wide[s, base : base + sub, :] = got[k, b, s, rows : rows + sub, :].astype(
                        jnp.float32
                    )
            return carry

        lax.fori_loop(0, stations, one, 0)

    def channels(k, start, stop):
        deep = 2 * blocks * per
        rows = pl.ds(k * deep if isinstance(k, int) else pl.multiple_of(k * deep, deep), deep)

        def channel(c, carry):
            flat, turned = channel_rows(wide, c, stations, blocks, own, local)
            both[c, rows, : stations * local] = flat
            both[c, rows, stations * local :] = turned
            return carry

        lax.fori_loop(start, stop, channel, 0, unroll=8)

    def arrange(k, carry):
        pltpu.make_async_copy(got.at[k], got.at[k], spec_recv.at[k]).wait()

        for half in range(halves):
            fill(k, half)

        half = blocks * own
        total = jnp.zeros((half, LANES), jnp.float32)
        for s in range(stations):
            re, im = wide[s, :half, :], wide[s, half:, :]
            total = total + (re * re + im * im)
        frame = lax.broadcasted_iota(jnp.int32, (frames, LANES), 0) - k * per
        pick = (lax.broadcasted_iota(jnp.int32, (frames, LANES), 1) // local == frame).astype(
            jnp.float32
        )
        power[...] += lax.dot_general(
            pick,
            total,
            (((1,), (1,)), ((), ())),
            precision=lax.Precision.HIGHEST,
            preferred_element_type=jnp.float32,
        )

        @pl.when(k == chunks - 2)
        def _():
            power_got[me_t] = power[...]
            for i in range(1, blocks):
                power_copy(i).start()

        channels(k, 0, own)
        return carry

    def power_copy(i):
        return pltpu.make_async_remote_copy(
            src_ref=power,
            dst_ref=power_got.at[me_t],
            send_sem=power_send.at[i],
            recv_sem=power_recv.at[i],
            device_id=(me_s, lax.rem(me_t + i, blocks)),
            device_id_type=MESH,
        )

    def tail_sum(which):
        pltpu.make_async_copy(tail_got.at[which], tail_got.at[which], tail_recv.at[which]).wait()
        total = tail_got[which, 0]
        for s in range(1, stations):
            total = total + tail_got[which, s]
        return total

    def tail_forward(target):
        return pltpu.make_async_remote_copy(
            src_ref=tail_next,
            dst_ref=tail_own,
            send_sem=tail_send.at[2],
            recv_sem=tail_recv.at[2],
            device_id=(me_s, target),
            device_id_type=MESH,
        )

    @pl.when(jnp.logical_not(last))
    def _():
        tail_next[...] = tail_sum(1)
        tail_forward(me_t + 1).start()

    lax.fori_loop(0, chunks - 1, arrange, 0)
    for half in range(halves):
        part = got.at[chunks - 1, :, :, pl.ds(half * 2 * sub, 2 * sub)]
        pltpu.make_async_copy(part, part, spec_recv.at[chunks - 1 + half]).wait()
        fill(chunks - 1, half)
        channels(chunks - 1, half * sub, (half + 1) * sub)

    for i in range(1, blocks):
        power_copy(i).wait()
    powers[...] = power_got[...]

    def tail_drain(which):
        sent = tail_out.at[which, pl.ds(0, stations - 1)]
        pltpu.make_async_copy(sent, sent, tail_send.at[which]).wait()

    @pl.when(first)
    def _():
        tail[...] = tail_sum(0)
        tail_drain(0)

    @pl.when(jnp.logical_not(first))
    def _():
        tail_forward(me_t).wait_recv()
        tail[...] = tail_own[...]

    @pl.when(jnp.logical_not(last))
    def _():
        tail_drain(1)
        tail_forward(me_t + 1).wait_send()

    def drain(job, carry):
        sent = spec.at[job, pl.ds(0, dests - 1)]
        pltpu.make_async_copy(sent, sent, spec_send.at[job]).wait()
        return carry

    lax.fori_loop(low, high, drain, 0)

    @pl.when(jnp.logical_not(first))
    def _():
        for k in range(chunks):
            halo(k, me_t - 1).wait_send()


def correlate_kernel(blocks, own, scale, group, per, both, powers, tail, vis, power, out, out_sem):
    inputs = both.shape[2] // 2
    buffers = out.shape[0]

    def store(step):
        slot = lax.rem(step, buffers)
        return pltpu.make_async_copy(
            out.at[slot], vis.at[pl.ds(step * group, group)], out_sem.at[slot]
        )

    def products(step, carry):
        slot = lax.rem(step, buffers)
        pl.when(step >= buffers)(lambda: store(step - buffers).wait())
        for g in range(group):
            c = step * group + g
            prod = lax.dot_general(
                both[c, :, :inputs],
                both[c],
                (((0,), (0,)), ((), ())),
                preferred_element_type=jnp.float32,
            )
            out[slot, g, 0] = prod[:, :inputs] * scale
            out[slot, g, 1] = prod[:, inputs:] * scale
        store(step).start()
        return carry

    steps = own // group
    lax.fori_loop(0, steps, products, 0)

    me = lax.axis_index("tm")
    wide = powers.shape[2]
    row = lax.broadcasted_iota(jnp.int32, (wide, wide), 0)
    col = lax.broadcasted_iota(jnp.int32, (wide, wide), 1)
    total = jnp.zeros(power.shape, jnp.float32)
    for b in range(blocks):
        move = jnp.logical_and(row - me * own == col - b * own, col // own == b)
        total = total + lax.dot_general(
            powers[b],
            move.astype(jnp.float32),
            (((1,), (0,)), ((), ())),
            precision=lax.Precision.HIGHEST,
            preferred_element_type=jnp.float32,
        )
    power[...] = total * (1.0 / inputs)
    power[power.shape[0] - per :, :] = tail[:per, :] * (1.0 / inputs)

    def drain(step, carry):
        store(step).wait()
        return carry

    lax.fori_loop(max(0, steps - buffers), steps, drain, 0)


def body(samples, history, taps):
    frames, local, frame_len = samples.shape
    span = taps.shape[0]
    stations, blocks = lax.axis_size("station"), lax.axis_size("tm")
    dests = stations * blocks
    inputs = stations * local
    own = frame_len // 2 // dests
    per = LANES // local
    chunks = frames // per
    depth = 2 * frames * blocks
    tail_rows = max(8, per)
    table = dft_table(stations, blocks, own, frame_len)
    hbm = pl.BlockSpec(memory_space=pltpu.HBM)
    vmem = pl.BlockSpec(memory_space=pltpu.VMEM)
    in_hbm = [pltpu.with_memory_space_constraint(x, pltpu.HBM) for x in (samples, history, taps)]
    both, powers, tail = pl.pallas_call(
        functools.partial(spectra_kernel, stations, blocks, own, local, frames, span),
        in_specs=[hbm, hbm, hbm, hbm],
        out_specs=[vmem, vmem, vmem],
        out_shape=[
            jax.ShapeDtypeStruct((own, depth, 2 * inputs), jnp.bfloat16),
            jax.ShapeDtypeStruct((blocks, frames, blocks * own), jnp.float32),
            jax.ShapeDtypeStruct((tail_rows, blocks * own), jnp.float32),
        ],
        scratch_shapes=[
            pltpu.VMEM((span - 1 + 2 * frames, local, frame_len), jnp.bfloat16),
            pltpu.VMEM(taps.shape, jnp.float32),
            pltpu.VMEM(table.shape, jnp.bfloat16),
            pltpu.VMEM((LANES, frame_len), jnp.bfloat16),
            pltpu.VMEM((2 * chunks, dests, 2 * own, LANES), jnp.bfloat16),
            pltpu.VMEM((chunks, blocks, stations, 2 * own, LANES), jnp.bfloat16),
            pltpu.VMEM((stations, 2 * blocks * own, LANES), jnp.float32),
            pltpu.VMEM((frames, blocks * own), jnp.float32),
            pltpu.VMEM((blocks, frames, blocks * own), jnp.float32),
            pltpu.VMEM((blocks, tail_rows, stations * own), jnp.float32),
            pltpu.VMEM((2, stations, tail_rows, blocks * own), jnp.float32),
            pltpu.VMEM((2, stations, tail_rows, blocks * own), jnp.float32),
            pltpu.VMEM((tail_rows, blocks * own), jnp.float32),
            pltpu.VMEM((tail_rows, blocks * own), jnp.float32),
            pltpu.SemaphoreType.DMA((3,)),
            pltpu.SemaphoreType.DMA((blocks,)),
            pltpu.SemaphoreType.DMA((chunks,)),
            pltpu.SemaphoreType.DMA((chunks,)),
            pltpu.SemaphoreType.DMA((2 * chunks,)),
            pltpu.SemaphoreType.DMA((chunks - 1 + halves_of(own),)),
            pltpu.SemaphoreType.DMA((blocks,)),
            pltpu.SemaphoreType.DMA((blocks,)),
            pltpu.SemaphoreType.DMA((3,)),
            pltpu.SemaphoreType.DMA((3,)),
        ],
        compiler_params=pltpu.CompilerParams(
            collective_id=0, has_side_effects=True, vmem_limit_bytes=VMEM_LIMIT
        ),
        cost_estimate=pl.CostEstimate(
            flops=8 * frames * local * frame_len * dests * own,
            bytes_accessed=8 * samples.size + table.size * 2,
            transcendentals=0,
        ),
    )(*in_hbm, table)

    group = math.gcd(own, 2)
    visibility, power = pl.pallas_call(
        functools.partial(correlate_kernel, blocks, own, 1.0 / (frames * blocks), group, per),
        in_specs=[vmem, vmem, vmem],
        out_specs=[pl.BlockSpec(memory_space=pl.ANY), vmem],
        out_shape=[
            jax.ShapeDtypeStruct((own, 2, inputs, inputs), jnp.float32),
            jax.ShapeDtypeStruct((frames, blocks * own), jnp.float32),
        ],
        scratch_shapes=[
            pltpu.VMEM((4, group, 2, inputs, inputs), jnp.float32),
            pltpu.SemaphoreType.DMA((4,)),
        ],
        compiler_params=pltpu.CompilerParams(vmem_limit_bytes=24 * 1024 * 1024),
    )(both, powers, tail)
    return visibility, power


def solution(mesh):
    return jax.shard_map(
        body,
        mesh=mesh,
        in_specs=(P("tm", "station", None), P(None, "station", None), P()),
        out_specs=(P(("station", "tm"), None, None, None), P("tm", "station")),
        check_vma=False,
    )
```

```python
import functools
import math

import jax
import jax.numpy as jnp
import numpy as np
from jax import lax
from jax.experimental import pallas as pl
from jax.experimental.pallas import tpu as pltpu
from jax.sharding import PartitionSpec as P

MESH = pl.DeviceIdType.MESH
LANES = 128
VMEM_LIMIT = 44 * 1024 * 1024


def halves_of(own):
    return 2 if own % 32 == 0 else 1


def dft_table(stations, blocks, own, frame_len):
    channel = np.arange(stations * blocks * own).reshape(stations, blocks, own)
    channel = channel.transpose(1, 0, 2).reshape(-1)
    phase = channel[:, None] * np.arange(frame_len)[None, :] % frame_len
    angle = phase.astype(np.float32) * np.float32(2.0 * math.pi / frame_len)
    parts = np.stack([np.cos(angle), -np.sin(angle)], axis=0)
    halves = halves_of(own)
    parts = parts.reshape(2, blocks * stations, halves, own // halves, frame_len)
    parts = parts.transpose(1, 2, 0, 3, 4)
    return jnp.asarray(parts.reshape(-1, frame_len).astype(jnp.bfloat16))


def channel_rows(wide, channel, stations, blocks, own, local):
    slots = LANES // local
    rows = 2 * blocks
    lane = lax.broadcasted_iota(jnp.int32, (rows, LANES), 1) // local
    sign = jnp.where(
        lax.broadcasted_iota(jnp.int32, (rows, stations * local), 0) < blocks, 1.0, -1.0
    )
    halves = []
    for h in range(stations // slots):
        parts = [
            wide[h * slots + s, pl.ds(channel, rows, stride=own), :] for s in range(slots)
        ]
        tiles = []
        for t in range(slots):
            tile = None
            for s in range(slots):
                shift = (s - t) % slots * local
                moved = parts[s] if shift == 0 else pltpu.roll(parts[s], shift, 1)
                tile = moved if tile is None else jnp.where(lane == s, moved, tile)
            tiles.append(tile)
        halves.append(tiles)
    flat, turned = [], []
    for t in range(slots):
        full = jnp.concatenate([half[t] for half in halves], axis=1)
        flat.append(full)
        turned.append(pltpu.roll(full, blocks, 0) * sign)
    flat = jnp.concatenate(flat, axis=0).astype(jnp.bfloat16)
    turned = jnp.concatenate(turned, axis=0).astype(jnp.bfloat16)
    return flat, turned


def spectra_kernel(
    stations, blocks, own, local, frames, span,
    samples, history, taps_hbm, table_hbm,
    both, powers, tail,
    ext, taps, table, weighted, spec, got, wide, power, power_out, power_got, tail_part, tail_out, tail_got, tail_next, tail_own,
    load_sem, table_sem, halo_send, halo_recv, spec_send, spec_recv, power_send, power_recv, tail_send, tail_recv,
):
    me_s, me_t = lax.axis_index("station"), lax.axis_index("tm")
    dests = stations * blocks
    halves = halves_of(own)
    sub = own // halves
    per = LANES // local
    chunks = frames // per
    frame_len = samples.shape[2]
    hist = span - 1
    first = me_t == 0
    last = me_t == blocks - 1

    load_own = pltpu.make_async_copy(samples, ext.at[pl.ds(hist, frames)], load_sem.at[0])
    load_hist = pltpu.make_async_copy(history, ext.at[pl.ds(0, hist)], load_sem.at[1])

    load_taps = pltpu.make_async_copy(taps_hbm, taps, load_sem.at[2])

    depth = stations * 2 * own

    def load_table(plane):
        rows = pl.ds(pl.multiple_of(plane * depth, depth), depth)
        return pltpu.make_async_copy(table_hbm.at[rows], table.at[rows], table_sem.at[plane])

    load_own.start()
    pl.when(first)(load_hist.start)
    load_taps.start()

    @pl.when(jnp.logical_not(last))
    def _():
        for plane in reversed(range(blocks)):
            load_table(plane).start()

    barrier = pltpu.get_barrier_semaphore()

    def greet(i, carry):
        other = lax.rem(me_s * blocks + me_t + i, dests)
        pl.semaphore_signal(
            barrier,
            inc=1,
            device_id=(other // blocks, lax.rem(other, blocks)),
            device_id_type=MESH,
        )
        return carry

    lax.fori_loop(1, dests, greet, 0)
    load_own.wait()
    load_taps.wait()

    def filter_chunk(start):
        def tile(i, carry):
            lanes = pl.ds(pl.multiple_of(i * LANES, LANES), LANES)
            sums = [None] * per
            for e in range(per + span - 1):
                x = ext[start + e, :, lanes].astype(jnp.float32)
                for j in range(per):
                    tap = j + span - 1 - e
                    if 0 <= tap < span:
                        term = taps[tap : tap + 1, lanes] * x
                        sums[j] = term if sums[j] is None else sums[j] + term
            for j in range(per):
                weighted[j * local : (j + 1) * local, lanes] = sums[j].astype(jnp.bfloat16)
            return carry

        lax.fori_loop(0, frame_len // LANES, tile, 0)

    @pl.when(first)
    def _():
        load_hist.wait()
        filter_chunk(0)

    pl.semaphore_wait(barrier, dests - 1)

    def halo(k, target):
        return pltpu.make_async_remote_copy(
            src_ref=samples.at[pl.ds(k * per, per)],
            dst_ref=ext.at[pl.ds(hist + frames + k * per, per)],
            send_sem=halo_send.at[k],
            recv_sem=halo_recv.at[k],
            device_id=(me_s, target),
            device_id_type=MESH,
        )

    @pl.when(jnp.logical_not(first))
    def _():
        for k in range(chunks):
            halo(k, me_t - 1).start()

    def send(job, plane, half=None):
        k = lax.rem(job, chunks)
        rows = pl.ds(0, 2 * own) if half is None else pl.ds(half * 2 * sub, 2 * sub)
        landed = spec_recv.at[k if half is None else k + half]
        block = jnp.where(job < chunks, 0, me_t + 1)

        def one(i, carry):
            s = lax.rem(me_s + i, stations)
            here = jnp.logical_and(i == 0, plane == me_t)
            piece = spec.at[job, plane * stations + s, rows]
            place = got.at[k, block, me_s, rows]

            @pl.when(here)
            def _():
                pltpu.make_async_copy(piece, place, landed).start()

            @pl.when(jnp.logical_not(here))
            def _():
                pltpu.make_async_remote_copy(
                    src_ref=piece,
                    dst_ref=place,
                    send_sem=spec_send.at[job],
                    recv_sem=landed,
                    device_id=(s, plane),
                    device_id_type=MESH,
                ).start()

            return carry

        lax.fori_loop(0, stations, one, 0)

    low = jnp.where(first, 0, chunks)
    high = jnp.where(last, chunks, 2 * chunks)

    def tail_copy(which, i):
        s = lax.rem(me_s + i, stations)
        return pltpu.make_async_remote_copy(
            src_ref=tail_out.at[which, s],
            dst_ref=tail_got.at[which, me_s],
            send_sem=tail_send.at[which],
            recv_sem=tail_recv.at[which],
            device_id=(s, me_t),
            device_id_type=MESH,
        )

    above = blocks - 1 - me_t
    lane_frame = lax.broadcasted_iota(jnp.int32, tail_out.shape[2:3] + (LANES,), 1) // local
    pick_tail = (
        lane_frame == lax.broadcasted_iota(jnp.int32, lane_frame.shape, 0)
    ).astype(jnp.float32)

    def work(job, carry):
        @pl.when(job >= chunks)
        def _():
            halo(job - chunks, me_t).wait_recv()

        pl.when(job > 0)(lambda: filter_chunk(job * per))

        closing = lax.rem(job, chunks) == chunks - 1

        def plane_of(i):
            return jnp.where(i < above, blocks - 1 - i, jnp.where(i < blocks - 1, i - above, me_t))

        def planes(i, carry):
            plane = plane_of(i)
            pl.when(job == low)(load_table(plane).wait)
            out = lax.dot_general(
                table[pl.ds(pl.multiple_of(plane * depth, depth), depth), :],
                weighted[...],
                (((1,), (1,)), ((), ())),
                preferred_element_type=jnp.float32,
            )
            out = out.astype(jnp.bfloat16).reshape(stations, 2 * own, LANES)
            spec[job, pl.ds(plane * stations, stations)] = out

            @pl.when(closing)
            def _():
                values = out.astype(jnp.float32)
                values = values * values
                values = values.reshape(stations * halves, 2 * sub, LANES)
                values = (values[:, :sub] + values[:, sub:]).reshape(stations * own, LANES)
                tail_part[plane] = lax.dot_general(
                    pick_tail,
                    values,
                    (((1,), (1,)), ((), ())),
                    precision=lax.Precision.HIGHEST,
                    preferred_element_type=jnp.float32,
                )

            near = jnp.logical_and(job < chunks - 1, plane == me_t + 1)
            now = jnp.logical_and(plane >= me_t, jnp.logical_not(near))
            pl.when(jnp.logical_and(now, jnp.logical_not(closing)))(lambda: send(job, plane))

            @pl.when(job == chunks - 1)
            def _():
                for half in range(halves):
                    send(job, plane, half)

            return carry

        lax.fori_loop(0, blocks, planes, 0)

        @pl.when(job == 2 * chunks - 2)
        def _():
            def older(old, carry):
                def plane_of(plane, carry):
                    send(old, plane)
                    return carry

                return lax.fori_loop(0, me_t, plane_of, carry)

            lax.fori_loop(chunks, 2 * chunks - 1, older, 0)

        @pl.when(job == 2 * chunks - 1)
        def _():
            for half in range(halves):

                def finish(i, carry):
                    send(job, plane_of(i), half)
                    return carry

                lax.fori_loop(0, blocks, finish, 0)

        @pl.when(job == chunks - 1)
        def _():
            def near(old, carry):
                send(old, me_t + 1)
                return carry

            lax.fori_loop(0, chunks - 1, near, 0)

        @pl.when(lax.rem(job, chunks) == chunks - 1)
        def _():
            which = job // chunks
            for s in range(stations):
                tail_out[which, s] = jnp.concatenate(
                    [tail_part[plane, :, s * own : (s + 1) * own] for plane in range(blocks)],
                    axis=1,
                )

            pltpu.make_async_copy(
                tail_out.at[which, me_s], tail_got.at[which, me_s], tail_recv.at[which]
            ).start()
            for i in range(1, stations):
                tail_copy(which, i).start()

        return carry

    lax.fori_loop(low, high, work, 0)

    power[...] = jnp.zeros_like(power)
    power_out[...] = jnp.zeros_like(power_out)

    def fill(k, half):
        def one(s, carry):
            for b in range(blocks):
                for p in range(2):
                    base = (p * blocks + b) * own + half * sub
                    rows = (half * 2 + p) * sub
                    wide[s, base : base + sub, :] = got[k, b, s, rows : rows + sub, :].astype(
                        jnp.float32
                    )
            return carry

        lax.fori_loop(0, stations, one, 0)

    def channels(k, start, stop):
        deep = 2 * blocks * per
        rows = pl.ds(k * deep if isinstance(k, int) else pl.multiple_of(k * deep, deep), deep)

        def channel(c, carry):
            flat, turned = channel_rows(wide, c, stations, blocks, own, local)
            both[c, rows, : stations * local] = flat
            both[c, rows, stations * local :] = turned
            return carry

        lax.fori_loop(start, stop, channel, 0, unroll=8)

    def arrange(k, carry):
        pltpu.make_async_copy(got.at[k], got.at[k], spec_recv.at[k]).wait()

        for half in range(halves):
            fill(k, half)

        half = blocks * own
        total = jnp.zeros((half, LANES), jnp.float32)
        for s in range(stations):
            re, im = wide[s, :half, :], wide[s, half:, :]
            total = total + (re * re + im * im)
        frame = lax.broadcasted_iota(jnp.int32, (frames, LANES), 0) - k * per
        pick = (lax.broadcasted_iota(jnp.int32, (frames, LANES), 1) // local == frame).astype(
            jnp.float32
        )
        power[...] += lax.dot_general(
            pick,
            total,
            (((1,), (1,)), ((), ())),
            precision=lax.Precision.HIGHEST,
            preferred_element_type=jnp.float32,
        )

        @pl.when(k == chunks - 2)
        def _():
            for b in range(blocks):
                power_out[b, :per, :] = jnp.concatenate(
                    [
                        power[j * per : (j + 1) * per, b * own : (b + 1) * own]
                        for j in range(chunks - 1)
                    ],
                    axis=1,
                )
            power_got[me_t] = power_out[me_t]
            for i in range(1, blocks):
                power_copy(i).start()

        channels(k, 0, own)
        return carry

    def power_copy(i):
        return pltpu.make_async_remote_copy(
            src_ref=power_out.at[lax.rem(me_t + i, blocks)],
            dst_ref=power_got.at[me_t],
            send_sem=power_send.at[i],
            recv_sem=power_recv.at[i],
            device_id=(me_s, lax.rem(me_t + i, blocks)),
            device_id_type=MESH,
        )

    def tail_sum(which):
        pltpu.make_async_copy(tail_got.at[which], tail_got.at[which], tail_recv.at[which]).wait()
        total = tail_got[which, 0]
        for s in range(1, stations):
            total = total + tail_got[which, s]
        return total

    def tail_forward(target):
        return pltpu.make_async_remote_copy(
            src_ref=tail_next,
            dst_ref=tail_own,
            send_sem=tail_send.at[2],
            recv_sem=tail_recv.at[2],
            device_id=(me_s, target),
            device_id_type=MESH,
        )

    @pl.when(jnp.logical_not(last))
    def _():
        tail_next[...] = tail_sum(1)
        tail_forward(me_t + 1).start()

    lax.fori_loop(0, chunks - 1, arrange, 0)
    for half in range(halves):
        part = got.at[chunks - 1, :, :, pl.ds(half * 2 * sub, 2 * sub)]
        pltpu.make_async_copy(part, part, spec_recv.at[chunks - 1 + half]).wait()
        fill(chunks - 1, half)
        channels(chunks - 1, half * sub, (half + 1) * sub)

    for i in range(1, blocks):
        power_copy(i).wait()
    powers[...] = power_got[...]

    def tail_drain(which):
        sent = tail_out.at[which, pl.ds(0, stations - 1)]
        pltpu.make_async_copy(sent, sent, tail_send.at[which]).wait()

    @pl.when(first)
    def _():
        tail[...] = tail_sum(0)
        tail_drain(0)

    @pl.when(jnp.logical_not(first))
    def _():
        tail_forward(me_t).wait_recv()
        tail[...] = tail_own[...]

    @pl.when(jnp.logical_not(last))
    def _():
        tail_drain(1)
        tail_forward(me_t + 1).wait_send()

    def drain(job, carry):
        sent = spec.at[job, pl.ds(0, dests - 1)]
        pltpu.make_async_copy(sent, sent, spec_send.at[job]).wait()
        return carry

    lax.fori_loop(low, high, drain, 0)

    @pl.when(jnp.logical_not(first))
    def _():
        for k in range(chunks):
            halo(k, me_t - 1).wait_send()


def correlate_kernel(blocks, own, scale, group, per, both, powers, tail, vis, power, out, out_sem):
    inputs = both.shape[2] // 2
    buffers = out.shape[0]

    def store(step):
        slot = lax.rem(step, buffers)
        return pltpu.make_async_copy(
            out.at[slot], vis.at[pl.ds(step * group, group)], out_sem.at[slot]
        )

    def products(step, carry):
        slot = lax.rem(step, buffers)
        pl.when(step >= buffers)(lambda: store(step - buffers).wait())
        for g in range(group):
            c = step * group + g
            prod = lax.dot_general(
                both[c, :, :inputs],
                both[c],
                (((0,), (0,)), ((), ())),
                preferred_element_type=jnp.float32,
            )
            out[slot, g, 0] = prod[:, :inputs] * scale
            out[slot, g, 1] = prod[:, inputs:] * scale
        store(step).start()
        return carry

    steps = own // group
    lax.fori_loop(0, steps, products, 0)

    for k in range(powers.shape[2] // own):
        rows = [powers[b, :per, k * own : (k + 1) * own] for b in range(blocks)]
        power[k * per : (k + 1) * per, :] = jnp.concatenate(rows, axis=1) * (1.0 / inputs)
    power[power.shape[0] - per :, :] = tail[:per, :] * (1.0 / inputs)

    def drain(step, carry):
        store(step).wait()
        return carry

    lax.fori_loop(max(0, steps - buffers), steps, drain, 0)


def body(samples, history, taps):
    frames, local, frame_len = samples.shape
    span = taps.shape[0]
    stations, blocks = lax.axis_size("station"), lax.axis_size("tm")
    dests = stations * blocks
    inputs = stations * local
    own = frame_len // 2 // dests
    per = LANES // local
    chunks = frames // per
    depth = 2 * frames * blocks
    tail_rows = max(8, per)
    table = dft_table(stations, blocks, own, frame_len)
    hbm = pl.BlockSpec(memory_space=pltpu.HBM)
    vmem = pl.BlockSpec(memory_space=pltpu.VMEM)
    in_hbm = [pltpu.with_memory_space_constraint(x, pltpu.HBM) for x in (samples, history, taps)]
    both, powers, tail = pl.pallas_call(
        functools.partial(spectra_kernel, stations, blocks, own, local, frames, span),
        in_specs=[hbm, hbm, hbm, hbm],
        out_specs=[vmem, vmem, vmem],
        out_shape=[
            jax.ShapeDtypeStruct((own, depth, 2 * inputs), jnp.bfloat16),
            jax.ShapeDtypeStruct((blocks, tail_rows, (chunks - 1) * own), jnp.float32),
            jax.ShapeDtypeStruct((tail_rows, blocks * own), jnp.float32),
        ],
        scratch_shapes=[
            pltpu.VMEM((span - 1 + 2 * frames, local, frame_len), jnp.bfloat16),
            pltpu.VMEM(taps.shape, jnp.float32),
            pltpu.VMEM(table.shape, jnp.bfloat16),
            pltpu.VMEM((LANES, frame_len), jnp.bfloat16),
            pltpu.VMEM((2 * chunks, dests, 2 * own, LANES), jnp.bfloat16),
            pltpu.VMEM((chunks, blocks, stations, 2 * own, LANES), jnp.bfloat16),
            pltpu.VMEM((stations, 2 * blocks * own, LANES), jnp.float32),
            pltpu.VMEM((frames, blocks * own), jnp.float32),
            pltpu.VMEM((blocks, tail_rows, (chunks - 1) * own), jnp.float32),
            pltpu.VMEM((blocks, tail_rows, (chunks - 1) * own), jnp.float32),
            pltpu.VMEM((blocks, tail_rows, stations * own), jnp.float32),
            pltpu.VMEM((2, stations, tail_rows, blocks * own), jnp.float32),
            pltpu.VMEM((2, stations, tail_rows, blocks * own), jnp.float32),
            pltpu.VMEM((tail_rows, blocks * own), jnp.float32),
            pltpu.VMEM((tail_rows, blocks * own), jnp.float32),
            pltpu.SemaphoreType.DMA((3,)),
            pltpu.SemaphoreType.DMA((blocks,)),
            pltpu.SemaphoreType.DMA((chunks,)),
            pltpu.SemaphoreType.DMA((chunks,)),
            pltpu.SemaphoreType.DMA((2 * chunks,)),
            pltpu.SemaphoreType.DMA((chunks - 1 + halves_of(own),)),
            pltpu.SemaphoreType.DMA((blocks,)),
            pltpu.SemaphoreType.DMA((blocks,)),
            pltpu.SemaphoreType.DMA((3,)),
            pltpu.SemaphoreType.DMA((3,)),
        ],
        compiler_params=pltpu.CompilerParams(
            collective_id=0, has_side_effects=True, vmem_limit_bytes=VMEM_LIMIT
        ),
        cost_estimate=pl.CostEstimate(
            flops=8 * frames * local * frame_len * dests * own,
            bytes_accessed=8 * samples.size + table.size * 2,
            transcendentals=0,
        ),
    )(*in_hbm, table)

    group = math.gcd(own, 2)
    visibility, power = pl.pallas_call(
        functools.partial(correlate_kernel, blocks, own, 1.0 / (frames * blocks), group, per),
        in_specs=[vmem, vmem, vmem],
        out_specs=[pl.BlockSpec(memory_space=pl.ANY), vmem],
        out_shape=[
            jax.ShapeDtypeStruct((own, 2, inputs, inputs), jnp.float32),
            jax.ShapeDtypeStruct((frames, blocks * own), jnp.float32),
        ],
        scratch_shapes=[
            pltpu.VMEM((4, group, 2, inputs, inputs), jnp.float32),
            pltpu.SemaphoreType.DMA((4,)),
        ],
        compiler_params=pltpu.CompilerParams(vmem_limit_bytes=24 * 1024 * 1024),
    )(both, powers, tail)
    return visibility, power


def solution(mesh):
    return jax.shard_map(
        body,
        mesh=mesh,
        in_specs=(P("tm", "station", None), P(None, "station", None), P()),
        out_specs=(P(("station", "tm"), None, None, None), P("tm", "station")),
        check_vma=False,
    )
```

```python
import functools
import math

import jax
import jax.numpy as jnp
import numpy as np
from jax import lax
from jax.experimental import pallas as pl
from jax.experimental.pallas import tpu as pltpu
from jax.sharding import PartitionSpec as P

MESH = pl.DeviceIdType.MESH
LANES = 128
VMEM_LIMIT = 44 * 1024 * 1024


def halves_of(own):
    return 2 if own % 32 == 0 else 1


def dft_table(stations, blocks, own, frame_len):
    channel = np.arange(stations * blocks * own).reshape(stations, blocks, own)
    channel = channel.transpose(1, 0, 2).reshape(-1)
    phase = channel[:, None] * np.arange(frame_len)[None, :] % frame_len
    angle = phase.astype(np.float32) * np.float32(2.0 * math.pi / frame_len)
    parts = np.stack([np.cos(angle), -np.sin(angle)], axis=0)
    halves = halves_of(own)
    parts = parts.reshape(2, blocks * stations, halves, own // halves, frame_len)
    parts = parts.transpose(1, 2, 0, 3, 4)
    return jnp.asarray(parts.reshape(-1, frame_len).astype(jnp.bfloat16))


def channel_rows(wide, channel, stations, blocks, own, local):
    slots = LANES // local
    rows = 2 * blocks
    lane = lax.broadcasted_iota(jnp.int32, (rows, LANES), 1) // local
    sign = jnp.where(
        lax.broadcasted_iota(jnp.int32, (rows, stations * local), 0) < blocks, 1.0, -1.0
    )
    halves = []
    for h in range(stations // slots):
        parts = [
            wide[h * slots + s, pl.ds(channel, rows, stride=own), :] for s in range(slots)
        ]
        tiles = []
        for t in range(slots):
            tile = None
            for s in range(slots):
                shift = (s - t) % slots * local
                moved = parts[s] if shift == 0 else pltpu.roll(parts[s], shift, 1)
                tile = moved if tile is None else jnp.where(lane == s, moved, tile)
            tiles.append(tile)
        halves.append(tiles)
    flat, turned = [], []
    for t in range(slots):
        full = jnp.concatenate([half[t] for half in halves], axis=1)
        flat.append(full)
        turned.append(pltpu.roll(full, blocks, 0) * sign)
    flat = jnp.concatenate(flat, axis=0).astype(jnp.bfloat16)
    turned = jnp.concatenate(turned, axis=0).astype(jnp.bfloat16)
    return flat, turned


def spectra_kernel(
    stations, blocks, own, local, frames, span,
    samples, history, taps_hbm, table_hbm,
    both, powers, tail,
    ext, taps, table, weighted, spec, got, wide, power, power_got, tail_part, tail_out, tail_got, tail_next, tail_own,
    load_sem, table_sem, halo_send, halo_recv, spec_send, spec_recv, power_send, power_recv, tail_send, tail_recv,
):
    me_s, me_t = lax.axis_index("station"), lax.axis_index("tm")
    dests = stations * blocks
    halves = halves_of(own)
    sub = own // halves
    per = LANES // local
    chunks = frames // per
    frame_len = samples.shape[2]
    hist = span - 1
    first = me_t == 0
    last = me_t == blocks - 1

    load_own = pltpu.make_async_copy(samples, ext.at[pl.ds(hist, frames)], load_sem.at[0])
    load_hist = pltpu.make_async_copy(history, ext.at[pl.ds(0, hist)], load_sem.at[1])

    load_taps = pltpu.make_async_copy(taps_hbm, taps, load_sem.at[2])

    depth = stations * 2 * own

    def load_table(plane):
        rows = pl.ds(pl.multiple_of(plane * depth, depth), depth)
        return pltpu.make_async_copy(table_hbm.at[rows], table.at[rows], table_sem.at[plane])

    load_own.start()
    pl.when(first)(load_hist.start)
    load_taps.start()

    @pl.when(jnp.logical_not(last))
    def _():
        for plane in reversed(range(blocks)):
            load_table(plane).start()

    barrier = pltpu.get_barrier_semaphore()

    def greet(i, carry):
        other = lax.rem(me_s * blocks + me_t + i, dests)
        pl.semaphore_signal(
            barrier,
            inc=1,
            device_id=(other // blocks, lax.rem(other, blocks)),
            device_id_type=MESH,
        )
        return carry

    lax.fori_loop(1, dests, greet, 0)
    load_own.wait()
    load_taps.wait()

    def filter_chunk(start):
        def tile(i, carry):
            lanes = pl.ds(pl.multiple_of(i * LANES, LANES), LANES)
            sums = [None] * per
            for e in range(per + span - 1):
                x = ext[start + e, :, lanes].astype(jnp.float32)
                for j in range(per):
                    tap = j + span - 1 - e
                    if 0 <= tap < span:
                        term = taps[tap : tap + 1, lanes] * x
                        sums[j] = term if sums[j] is None else sums[j] + term
            for j in range(per):
                weighted[j * local : (j + 1) * local, lanes] = sums[j].astype(jnp.bfloat16)
            return carry

        lax.fori_loop(0, frame_len // LANES, tile, 0)

    @pl.when(first)
    def _():
        load_hist.wait()
        filter_chunk(0)

    pl.semaphore_wait(barrier, dests - 1)

    def halo(k, target):
        return pltpu.make_async_remote_copy(
            src_ref=samples.at[pl.ds(k * per, per)],
            dst_ref=ext.at[pl.ds(hist + frames + k * per, per)],
            send_sem=halo_send.at[k],
            recv_sem=halo_recv.at[k],
            device_id=(me_s, target),
            device_id_type=MESH,
        )

    @pl.when(jnp.logical_not(first))
    def _():
        for k in range(chunks):
            halo(k, me_t - 1).start()

    def send(job, plane, half=None):
        k = lax.rem(job, chunks)
        rows = pl.ds(0, 2 * own) if half is None else pl.ds(half * 2 * sub, 2 * sub)
        landed = spec_recv.at[k if half is None else k + half]
        block = jnp.where(job < chunks, 0, me_t + 1)

        def one(i, carry):
            s = lax.rem(me_s + i, stations)
            here = jnp.logical_and(i == 0, plane == me_t)
            piece = spec.at[job, plane * stations + s, rows]
            place = got.at[k, block, me_s, rows]

            @pl.when(here)
            def _():
                pltpu.make_async_copy(piece, place, landed).start()

            @pl.when(jnp.logical_not(here))
            def _():
                pltpu.make_async_remote_copy(
                    src_ref=piece,
                    dst_ref=place,
                    send_sem=spec_send.at[job],
                    recv_sem=landed,
                    device_id=(s, plane),
                    device_id_type=MESH,
                ).start()

            return carry

        lax.fori_loop(0, stations, one, 0)

    low = jnp.where(first, 0, chunks)
    high = jnp.where(last, chunks, 2 * chunks)

    def tail_copy(which, i):
        s = lax.rem(me_s + i, stations)
        return pltpu.make_async_remote_copy(
            src_ref=tail_out.at[which, s],
            dst_ref=tail_got.at[which, me_s],
            send_sem=tail_send.at[which],
            recv_sem=tail_recv.at[which],
            device_id=(s, me_t),
            device_id_type=MESH,
        )

    above = blocks - 1 - me_t
    lane_frame = lax.broadcasted_iota(jnp.int32, tail_out.shape[2:3] + (LANES,), 1) // local
    pick_tail = (
        lane_frame == lax.broadcasted_iota(jnp.int32, lane_frame.shape, 0)
    ).astype(jnp.float32)

    def work(job, carry):
        @pl.when(job >= chunks)
        def _():
            halo(job - chunks, me_t).wait_recv()

        pl.when(job > 0)(lambda: filter_chunk(job * per))

        closing = lax.rem(job, chunks) == chunks - 1

        def plane_of(i):
            return jnp.where(i < above, blocks - 1 - i, jnp.where(i < blocks - 1, i - above, me_t))

        def planes(i, carry):
            plane = plane_of(i)
            pl.when(job == low)(load_table(plane).wait)
            out = lax.dot_general(
                table[pl.ds(pl.multiple_of(plane * depth, depth), depth), :],
                weighted[...],
                (((1,), (1,)), ((), ())),
                preferred_element_type=jnp.float32,
            )
            out = out.astype(jnp.bfloat16).reshape(stations, 2 * own, LANES)
            spec[job, pl.ds(plane * stations, stations)] = out

            @pl.when(closing)
            def _():
                values = out.astype(jnp.float32)
                values = values * values
                values = values.reshape(stations * halves, 2 * sub, LANES)
                values = (values[:, :sub] + values[:, sub:]).reshape(stations * own, LANES)
                tail_part[plane] = lax.dot_general(
                    pick_tail,
                    values,
                    (((1,), (1,)), ((), ())),
                    precision=lax.Precision.HIGHEST,
                    preferred_element_type=jnp.float32,
                )

            near = jnp.logical_and(job < chunks - 1, plane == me_t + 1)
            now = jnp.logical_and(plane >= me_t, jnp.logical_not(near))
            pl.when(jnp.logical_and(now, jnp.logical_not(closing)))(lambda: send(job, plane))

            @pl.when(job == chunks - 1)
            def _():
                for half in range(halves):
                    send(job, plane, half)

            pl.when(job == 2 * chunks - 1)(lambda: send(job, plane, 0))

            return carry

        lax.fori_loop(0, blocks, planes, 0)

        @pl.when(job == 2 * chunks - 2)
        def _():
            def older(old, carry):
                def plane_of(plane, carry):
                    send(old, plane)
                    return carry

                return lax.fori_loop(0, me_t, plane_of, carry)

            lax.fori_loop(chunks, 2 * chunks - 1, older, 0)

        @pl.when(job == 2 * chunks - 1)
        def _():
            for half in range(1, halves):

                def finish(i, carry):
                    send(job, plane_of(i), half)
                    return carry

                lax.fori_loop(0, blocks, finish, 0)

        @pl.when(jnp.logical_and(first, job == chunks))
        def _():
            def near(old, carry):
                send(old, me_t + 1)
                return carry

            lax.fori_loop(0, chunks - 1, near, 0)

        @pl.when(lax.rem(job, chunks) == chunks - 1)
        def _():
            which = job // chunks
            for s in range(stations):
                tail_out[which, s] = jnp.concatenate(
                    [tail_part[plane, :, s * own : (s + 1) * own] for plane in range(blocks)],
                    axis=1,
                )

            pltpu.make_async_copy(
                tail_out.at[which, me_s], tail_got.at[which, me_s], tail_recv.at[which]
            ).start()
            for i in range(1, stations):
                tail_copy(which, i).start()

        return carry

    lax.fori_loop(low, high, work, 0)

    power[...] = jnp.zeros_like(power)

    def fill(k, half):
        def one(s, carry):
            for b in range(blocks):
                for p in range(2):
                    base = (p * blocks + b) * own + half * sub
                    rows = (half * 2 + p) * sub
                    wide[s, base : base + sub, :] = got[k, b, s, rows : rows + sub, :].astype(
                        jnp.float32
                    )
            return carry

        lax.fori_loop(0, stations, one, 0)

    def channels(k, start, stop):
        deep = 2 * blocks * per
        rows = pl.ds(k * deep if isinstance(k, int) else pl.multiple_of(k * deep, deep), deep)

        def channel(c, carry):
            flat, turned = channel_rows(wide, c, stations, blocks, own, local)
            both[c, rows, : stations * local] = flat
            both[c, rows, stations * local :] = turned
            return carry

        lax.fori_loop(start, stop, channel, 0, unroll=min(16, stop - start))

    def arrange(k, carry):
        pltpu.make_async_copy(got.at[k], got.at[k], spec_recv.at[k]).wait()

        for half in range(halves):
            fill(k, half)

        half = blocks * own
        total = jnp.zeros((half, LANES), jnp.float32)
        for s in range(stations):
            re, im = wide[s, :half, :], wide[s, half:, :]
            total = total + (re * re + im * im)
        frame = lax.broadcasted_iota(jnp.int32, (frames, LANES), 0) - k * per
        pick = (lax.broadcasted_iota(jnp.int32, (frames, LANES), 1) // local == frame).astype(
            jnp.float32
        )
        power[...] += lax.dot_general(
            pick,
            total,
            (((1,), (1,)), ((), ())),
            precision=lax.Precision.HIGHEST,
            preferred_element_type=jnp.float32,
        )

        @pl.when(k == chunks - 2)
        def _():
            power_got[me_t] = power[...]
            for i in range(1, blocks):
                power_copy(i).start()

        channels(k, 0, own)
        return carry

    def power_copy(i):
        return pltpu.make_async_remote_copy(
            src_ref=power,
            dst_ref=power_got.at[me_t],
            send_sem=power_send.at[i],
            recv_sem=power_recv.at[i],
            device_id=(me_s, lax.rem(me_t + i, blocks)),
            device_id_type=MESH,
        )

    def tail_sum(which):
        pltpu.make_async_copy(tail_got.at[which], tail_got.at[which], tail_recv.at[which]).wait()
        total = tail_got[which, 0]
        for s in range(1, stations):
            total = total + tail_got[which, s]
        return total

    def tail_forward(target):
        return pltpu.make_async_remote_copy(
            src_ref=tail_next,
            dst_ref=tail_own,
            send_sem=tail_send.at[2],
            recv_sem=tail_recv.at[2],
            device_id=(me_s, target),
            device_id_type=MESH,
        )

    @pl.when(jnp.logical_not(last))
    def _():
        tail_next[...] = tail_sum(1)
        tail_forward(me_t + 1).start()

    lax.fori_loop(0, chunks - 1, arrange, 0)
    for half in range(halves):
        part = got.at[chunks - 1, :, :, pl.ds(half * 2 * sub, 2 * sub)]
        pltpu.make_async_copy(part, part, spec_recv.at[chunks - 1 + half]).wait()
        fill(chunks - 1, half)
        channels(chunks - 1, half * sub, (half + 1) * sub)

    for i in range(1, blocks):
        power_copy(i).wait()
    powers[...] = power_got[...]

    def tail_drain(which):
        sent = tail_out.at[which, pl.ds(0, stations - 1)]
        pltpu.make_async_copy(sent, sent, tail_send.at[which]).wait()

    @pl.when(first)
    def _():
        tail[...] = tail_sum(0)
        tail_drain(0)

    @pl.when(jnp.logical_not(first))
    def _():
        tail_forward(me_t).wait_recv()
        tail[...] = tail_own[...]

    @pl.when(jnp.logical_not(last))
    def _():
        tail_drain(1)
        tail_forward(me_t + 1).wait_send()

    def drain(job, carry):
        sent = spec.at[job, pl.ds(0, dests - 1)]
        pltpu.make_async_copy(sent, sent, spec_send.at[job]).wait()
        return carry

    lax.fori_loop(low, high, drain, 0)

    @pl.when(jnp.logical_not(first))
    def _():
        for k in range(chunks):
            halo(k, me_t - 1).wait_send()


def correlate_kernel(blocks, own, scale, group, per, both, powers, tail, vis, power, out, out_sem):
    inputs = both.shape[2] // 2
    buffers = out.shape[0]

    def store(step):
        slot = lax.rem(step, buffers)
        return pltpu.make_async_copy(
            out.at[slot], vis.at[pl.ds(step * group, group)], out_sem.at[slot]
        )

    def products(step, carry):
        slot = lax.rem(step, buffers)
        pl.when(step >= buffers)(lambda: store(step - buffers).wait())
        for g in range(group):
            c = step * group + g
            prod = lax.dot_general(
                both[c, :, :inputs],
                both[c],
                (((0,), (0,)), ((), ())),
                preferred_element_type=jnp.float32,
            )
            out[slot, g, 0] = prod[:, :inputs] * scale
            out[slot, g, 1] = prod[:, inputs:] * scale
        store(step).start()
        return carry

    steps = own // group
    lax.fori_loop(0, steps, products, 0)

    me = lax.axis_index("tm")
    wide = powers.shape[2]
    row = lax.broadcasted_iota(jnp.int32, (wide, wide), 0)
    col = lax.broadcasted_iota(jnp.int32, (wide, wide), 1)
    total = jnp.zeros(power.shape, jnp.float32)
    for b in range(blocks):
        move = jnp.logical_and(row - me * own == col - b * own, col // own == b)
        total = total + lax.dot_general(
            powers[b],
            move.astype(jnp.float32),
            (((1,), (0,)), ((), ())),
            precision=lax.Precision.HIGHEST,
            preferred_element_type=jnp.float32,
        )
    power[...] = total * (1.0 / inputs)
    power[power.shape[0] - per :, :] = tail[:per, :] * (1.0 / inputs)

    def drain(step, carry):
        store(step).wait()
        return carry

    lax.fori_loop(max(0, steps - buffers), steps, drain, 0)


def body(samples, history, taps):
    frames, local, frame_len = samples.shape
    span = taps.shape[0]
    stations, blocks = lax.axis_size("station"), lax.axis_size("tm")
    dests = stations * blocks
    inputs = stations * local
    own = frame_len // 2 // dests
    per = LANES // local
    chunks = frames // per
    depth = 2 * frames * blocks
    tail_rows = max(8, per)
    table = dft_table(stations, blocks, own, frame_len)
    hbm = pl.BlockSpec(memory_space=pltpu.HBM)
    vmem = pl.BlockSpec(memory_space=pltpu.VMEM)
    in_hbm = [pltpu.with_memory_space_constraint(x, pltpu.HBM) for x in (samples, history, taps)]
    both, powers, tail = pl.pallas_call(
        functools.partial(spectra_kernel, stations, blocks, own, local, frames, span),
        in_specs=[hbm, hbm, hbm, hbm],
        out_specs=[vmem, vmem, vmem],
        out_shape=[
            jax.ShapeDtypeStruct((own, depth, 2 * inputs), jnp.bfloat16),
            jax.ShapeDtypeStruct((blocks, frames, blocks * own), jnp.float32),
            jax.ShapeDtypeStruct((tail_rows, blocks * own), jnp.float32),
        ],
        scratch_shapes=[
            pltpu.VMEM((span - 1 + 2 * frames, local, frame_len), jnp.bfloat16),
            pltpu.VMEM(taps.shape, jnp.float32),
            pltpu.VMEM(table.shape, jnp.bfloat16),
            pltpu.VMEM((LANES, frame_len), jnp.bfloat16),
            pltpu.VMEM((2 * chunks, dests, 2 * own, LANES), jnp.bfloat16),
            pltpu.VMEM((chunks, blocks, stations, 2 * own, LANES), jnp.bfloat16),
            pltpu.VMEM((stations, 2 * blocks * own, LANES), jnp.float32),
            pltpu.VMEM((frames, blocks * own), jnp.float32),
            pltpu.VMEM((blocks, frames, blocks * own), jnp.float32),
            pltpu.VMEM((blocks, tail_rows, stations * own), jnp.float32),
            pltpu.VMEM((2, stations, tail_rows, blocks * own), jnp.float32),
            pltpu.VMEM((2, stations, tail_rows, blocks * own), jnp.float32),
            pltpu.VMEM((tail_rows, blocks * own), jnp.float32),
            pltpu.VMEM((tail_rows, blocks * own), jnp.float32),
            pltpu.SemaphoreType.DMA((3,)),
            pltpu.SemaphoreType.DMA((blocks,)),
            pltpu.SemaphoreType.DMA((chunks,)),
            pltpu.SemaphoreType.DMA((chunks,)),
            pltpu.SemaphoreType.DMA((2 * chunks,)),
            pltpu.SemaphoreType.DMA((chunks - 1 + halves_of(own),)),
            pltpu.SemaphoreType.DMA((blocks,)),
            pltpu.SemaphoreType.DMA((blocks,)),
            pltpu.SemaphoreType.DMA((3,)),
            pltpu.SemaphoreType.DMA((3,)),
        ],
        compiler_params=pltpu.CompilerParams(
            collective_id=0, has_side_effects=True, vmem_limit_bytes=VMEM_LIMIT
        ),
        cost_estimate=pl.CostEstimate(
            flops=8 * frames * local * frame_len * dests * own,
            bytes_accessed=8 * samples.size + table.size * 2,
            transcendentals=0,
        ),
    )(*in_hbm, table)

    group = math.gcd(own, 2)
    visibility, power = pl.pallas_call(
        functools.partial(correlate_kernel, blocks, own, 1.0 / (frames * blocks), group, per),
        in_specs=[vmem, vmem, vmem],
        out_specs=[pl.BlockSpec(memory_space=pl.ANY), vmem],
        out_shape=[
            jax.ShapeDtypeStruct((own, 2, inputs, inputs), jnp.float32),
            jax.ShapeDtypeStruct((frames, blocks * own), jnp.float32),
        ],
        scratch_shapes=[
            pltpu.VMEM((4, group, 2, inputs, inputs), jnp.float32),
            pltpu.SemaphoreType.DMA((4,)),
        ],
        compiler_params=pltpu.CompilerParams(vmem_limit_bytes=24 * 1024 * 1024),
    )(both, powers, tail)
    return visibility, power


def solution(mesh):
    return jax.shard_map(
        body,
        mesh=mesh,
        in_specs=(P("tm", "station", None), P(None, "station", None), P()),
        out_specs=(P(("station", "tm"), None, None, None), P("tm", "station")),
        check_vma=False,
    )
```
